32 devices in a mesh: fsdp: 2 (over y), tensor: 4 (over x, core), replica: 4 (over z).
Axes of the slice: x: 2, y: 2, z: 4, core: 2. Of those that a mesh axis runs over, the one named last changes fastest.
Arguments:
- gradient: bfloat16 [4, 4096, 8192], P('replica', 'fsdp', 'tensor'), may hold values from -400 to 400, as said below
- momentum: float32 [4, 4096, 8192], P('replica', 'fsdp', 'tensor'), may hold values from -6 to 6
- basis: float32 [8192, 256], P('tensor', 'fsdp'), may hold values from -0.0625 to 0.0625
Outputs:
- update: bfloat16 [4096, 8192], P('fsdp', 'tensor')
- momentum_new: float32 [4, 4096, 8192], P('replica', 'fsdp', 'tensor')
- basis_new: float32 [8192, 256], P('tensor', 'fsdp')
The draws below stay inside these ranges and needn't reach their ends.
Inputs may be any that keep to these rules, and one draw needn't show every extreme that they name: gradient entries are finite real numbers.
All inputs are finite; a program needn't handle non-finite values.
Results may differ from the reference program's by a relative error of at most 0.001.
Values sent between devices are 32-bit elements; how exact they have to be, the bound alone decides.
A program may use at most 128 MiB of HBM per device.

```python
import math
import jax
import jax.numpy as jnp
from jax import lax

M_ROWS = 4096
NCOLS = 8192
RANK = 256
REPL = 4


def draw_gradient(key, part):
    key_rows, key_cols, key_own = jax.random.split(key, 3)
    rows = jnp.exp(jax.random.uniform(key_rows, (1, M_ROWS, 1), jnp.float32) * math.log(10.0))
    rising = jnp.exp(jnp.arange(NCOLS, dtype=jnp.float32) / NCOLS * math.log(3.0))
    rough = jnp.exp(jax.random.uniform(key_cols, (NCOLS,), jnp.float32, -math.log(2.0), math.log(2.0)))
    cols = (rising * rough).reshape(1, 1, NCOLS)
    base = jax.random.truncated_normal(key_own, -6.0, 6.0, (REPL, M_ROWS, NCOLS), jnp.float32)
    return (base * rows * cols).astype(jnp.bfloat16)


def steps_of(rng, dims, pieces, smallest, largest):
    gain = 1.0
    for position, shards_of in pieces:
        draws = jax.random.uniform(jax.random.fold_in(jax.random.fold_in(rng, 6), position), (shards_of,), jnp.float32, smallest / len(pieces), largest / len(pieces))
        gain = gain * jnp.repeat(jnp.exp(draws), dims[position] // shards_of).reshape((-1,) + (1,) * (len(dims) - 1 - position))
    return gain


def noise(stream_key, shape, scale, most, shards=(), kind=jnp.bfloat16):
    level = steps_of(stream_key, shape, shards, -0.22, 0.18) if shards else 1.0
    array = jax.random.normal(stream_key, shape, jnp.float32) * scale * level
    return jnp.minimum(jnp.maximum(array, -most), most).astype(kind)


def setup_inputs(seed: int = 0) -> dict:
    arg_keys = jax.random.split(jax.random.key(seed), 4)
    return {
        "gradient": draw_gradient(jax.random.fold_in(arg_keys[3], 71), 0),
        "momentum": noise(arg_keys[1], (REPL, M_ROWS, NCOLS), 1.0, 6.0, ((0, 4), (1, 2), (2, 4)), jnp.float32),
        "basis": noise(arg_keys[2], (NCOLS, RANK), NCOLS ** -0.5, 0.0625, ((0, 4), (1, 2)), jnp.float32),
    }


HIGH = lax.Precision.HIGHEST

def reference(gradient, momentum, basis):
    count = gradient.shape[0]

    def left_term(index):
        buffer = momentum[index] + gradient[index].astype(jnp.float32)
        return jnp.dot(buffer.astype(jnp.float32), basis.astype(jnp.float32), precision=HIGH, preferred_element_type=jnp.float32)
    left = lax.optimization_barrier(jnp.sum(lax.map(left_term, jnp.arange(count)), axis=0)) / count
    gram = jnp.dot(left.T.astype(jnp.float32), left.astype(jnp.float32), precision=HIGH, preferred_element_type=jnp.float32)
    chol = jnp.linalg.cholesky(gram)
    ortho = lax.linalg.triangular_solve(chol, left, left_side=False, lower=True, transpose_a=True)

    def right_term(index):
        buffer = momentum[index] + gradient[index].astype(jnp.float32)
        return jnp.dot(buffer.T.astype(jnp.float32), ortho.astype(jnp.float32), precision=HIGH, preferred_element_type=jnp.float32)
    right = lax.optimization_barrier(jnp.sum(lax.map(right_term, jnp.arange(count)), axis=0)) / count
    norms = jnp.sqrt(lax.optimization_barrier(jnp.sum(right * right, axis=0)) + 1e-12)
    basis_new = right / norms
    lowrank = jnp.dot(ortho.astype(jnp.float32), right.T.astype(jnp.float32), precision=HIGH, preferred_element_type=jnp.float32)

    def feedback(index):
        buffer = momentum[index] + gradient[index].astype(jnp.float32)
        return buffer - 0.05 * lowrank
    momentum_new = lax.map(feedback, jnp.arange(count))
    scale = (M_ROWS * NCOLS / RANK) ** 0.5
    update = (scale * jnp.dot(ortho.astype(jnp.float32), basis_new.T.astype(jnp.float32), precision=HIGH, preferred_element_type=jnp.float32)).astype(jnp.bfloat16)
    return (update, momentum_new, basis_new)
```

```python
import functools

import jax
import jax.numpy as jnp
from jax import lax
from jax.experimental import pallas as pl
from jax.experimental.pallas import tpu as pltpu
from jax.sharding import PartitionSpec as P

HIGHEST = lax.Precision.HIGHEST
HIGH = lax.Precision.HIGH
BLOCK = 16


def mm(a, b, precision):
    return jnp.dot(a, b, precision=precision, preferred_element_type=jnp.float32)


def pick(parts, index):
    return lax.dynamic_index_in_dim(parts, index, 0, keepdims=False)


def shift(x, axis, step):
    n = lax.axis_size(axis)
    return lax.ppermute(x, axis, [(i, (i + step) % n) for i in range(n)])


def swap(x, axis, bit):
    n = lax.axis_size(axis)
    return lax.ppermute(x, axis, [(i, i ^ bit) for i in range(n)])


def bits_of(axis):
    n = lax.axis_size(axis)
    bits, bit = [], 1
    while bit < n:
        bits.append(bit)
        bit *= 2
    return bits


def halve(x, axis, bits):
    for bit in bits:
        upper = (lax.axis_index(axis) // bit) % 2
        parts = x.reshape(2, x.shape[0] // 2, x.shape[1])
        x = pick(parts, upper) + swap(pick(parts, 1 - upper), axis, bit)
    return x


def double(x, axis, bits):
    for bit in reversed(bits):
        upper = (lax.axis_index(axis) // bit) % 2 == 1
        other = swap(x, axis, bit)
        x = jnp.concatenate([jnp.where(upper, other, x), jnp.where(upper, x, other)], axis=0)
    return x


def ring_scatter(x, axis):
    n = lax.axis_size(axis)
    me = lax.axis_index(axis)
    parts = x.reshape(n, 2, x.shape[0] // (2 * n), x.shape[1])
    up, down = parts[:, 0], parts[:, 1]
    a, b = pick(up, (me + n - 1) % n), pick(down, (me + 1) % n)
    for step in range(n - 1):
        a = shift(a, axis, 1) + pick(up, (me + 2 * n - step - 2) % n)
        b = shift(b, axis, n - 1) + pick(down, (me + step + 2) % n)
    return jnp.concatenate([a, b], axis=0)


def ring_gather(x, axis):
    n = lax.axis_size(axis)
    me = lax.axis_index(axis)
    half = x.shape[0] // 2
    a, b = x[:half], x[half:]
    out = jnp.zeros((n, 2, half, x.shape[1]), x.dtype)

    def put(out, value, chunk, side):
        return lax.dynamic_update_slice(out, value[None, None], (chunk, side, 0, 0))

    out = put(put(out, a, me, 0), b, me, 1)
    for step in range(n - 1):
        a = shift(a, axis, 1)
        b = shift(b, axis, n - 1)
        out = put(out, a, (me + n - step - 1) % n, 0)
        out = put(out, b, (me + step + 1) % n, 1)
    return out.reshape(n * x.shape[0], x.shape[1])


def sum_over(x, axis, bits, ring):
    half = x.shape[0] // 2
    first = ring_scatter(halve(x[:half], axis, bits), ring)
    second = halve(ring_scatter(x[half:], ring), axis, bits)
    first = double(ring_gather(first, ring), axis, bits)
    second = ring_gather(double(second, axis, bits), ring)
    return jnp.concatenate([first, second], axis=0)


def invert_kernel(gram_ref, out_ref, work):
    size = gram_ref.shape[0]
    rows = lax.broadcasted_iota(jnp.int32, (size, size), 0)
    cols = lax.broadcasted_iota(jnp.int32, (size, size), 1)
    work[:, :size] = gram_ref[...]
    work[:, size:] = jnp.where(rows == cols, 1.0, 0.0).astype(jnp.float32)
    lane = lax.broadcasted_iota(jnp.int32, (BLOCK, 2 * size), 1)
    row = lax.broadcasted_iota(jnp.int32, (BLOCK, 2 * size), 0)
    below = lax.broadcasted_iota(jnp.int32, (BLOCK, 1), 0)
    for start in range(0, size, BLOCK):
        panel = work[start : start + BLOCK, :]
        for j in range(BLOCK):
            column = start + j
            factor = panel[:, column : column + 1] / panel[j : j + 1, column : column + 1]
            factor = jnp.where(below > j, factor, 0.0)
            panel = panel - factor * panel[j : j + 1, :]
        pivots = jnp.sum(jnp.where(lane == row + start, panel, 0.0), axis=1, keepdims=True)
        panel = panel / jnp.sqrt(pivots)
        out_ref[start : start + BLOCK, :] = panel[:, size:]
        if start + BLOCK < size:
            outer = lax.dot_general(
                panel[:, :size],
                panel,
                (((0,), (0,)), ((), ())),
                precision=HIGHEST,
                preferred_element_type=jnp.float32,
            )
            work[start + BLOCK :, :] = work[start + BLOCK :, :] - outer[start + BLOCK :, :]


def inverse_factor(gram, interpret=False):
    size = gram.shape[0]
    return pl.pallas_call(
        invert_kernel,
        out_shape=jax.ShapeDtypeStruct((size, size), jnp.float32),
        in_specs=[pl.BlockSpec(memory_space=pltpu.VMEM)],
        out_specs=pl.BlockSpec(memory_space=pltpu.VMEM),
        scratch_shapes=[pltpu.VMEM((size, 2 * size), jnp.float32)],
        interpret=interpret,
    )(gram)


def gather_columns(x, axis):
    for bit in bits_of(axis):
        upper = (lax.axis_index(axis) // bit) % 2 == 1
        other = swap(x, axis, bit)
        x = jnp.concatenate([jnp.where(upper, other, x), jnp.where(upper, x, other)], axis=1)
    return x


def local(gradient, momentum, basis):
    replicas = lax.axis_size("replica")
    rank_local = basis.shape[1]
    rank = rank_local * lax.axis_size("fsdp")
    rows = gradient.shape[1] * lax.axis_size("fsdp")
    columns = gradient.shape[2] * lax.axis_size("tensor")
    buffer = momentum[0] + gradient[0].astype(jnp.float32)

    left = mm(buffer, gather_columns(basis, "fsdp"), HIGH)
    bits = bits_of("tensor")
    left = halve(left, "tensor", bits[:1])
    left = sum_over(left, "tensor", bits[1:], "replica")
    left = double(left, "tensor", bits[:1]) / replicas

    gram = mm(left.T, left, HIGHEST)
    for bit in bits_of("fsdp"):
        gram = gram + swap(gram, "fsdp", bit)
    ortho = mm(left, inverse_factor(gram).T, HIGHEST)

    right = mm(buffer.T, ortho, HIGH)
    right = sum_over(right, "fsdp", bits_of("fsdp"), "replica") / replicas
    squares = jnp.sum(right * right, axis=0, keepdims=True)
    for bit in bits_of("tensor"):
        squares = squares + swap(squares, "tensor", bit)
    norms = jnp.sqrt(squares + 1e-12)
    basis_full = right / norms
    lowrank = mm(ortho, right.T, lax.Precision.DEFAULT)
    momentum_new = (buffer - 0.05 * lowrank)[None]
    scale = (rows * columns / rank) ** 0.5
    update = (scale * mm(ortho, basis_full.T, HIGH)).astype(jnp.bfloat16)
    offset = lax.axis_index("fsdp") * rank_local
    basis_new = lax.dynamic_slice_in_dim(basis_full, offset, rank_local, 1)
    return (update, momentum_new, basis_new)

MESH = pl.DeviceIdType.MESH
SLABS = 4
FEEDS = 8
WIDTH = 256
GAP = 2
PANEL = 16
VMEM = pltpu.VMEM
ANY = pl.ANY


def dot(a, b, precision=None):
    return jnp.dot(a, b, precision=precision, preferred_element_type=jnp.float32)


def split(x):
    high = x.astype(jnp.bfloat16)
    return high, (x - high.astype(jnp.float32)).astype(jnp.bfloat16)


def rows_of(start, size, unit=8):
    return pl.ds(pl.multiple_of(start, unit), size)


class Line:
    def __init__(self):
        self.n = lax.axis_size("replica")
        self.half = self.n // 2
        me = lax.axis_index("replica")
        low = me < self.half
        self.me = me
        self.depth = jnp.where(low, me, self.n - 1 - me)
        self.inward = {"replica": jnp.where(low, me + 1, me - 1)}
        outward = jnp.where(low, me - 1, me + 1)
        self.outward = {"replica": jnp.where(self.depth > 0, outward, self.inward["replica"])}


def remote(src, dst, send, recv, device):
    return pltpu.make_async_remote_copy(
        src_ref=src, dst_ref=dst, send_sem=send, recv_sem=recv, device_id=device, device_id_type=MESH
    )


def panel_step(work, out, start):
    size = out.shape[0]
    lane = lax.broadcasted_iota(jnp.int32, (PANEL, 2 * size), 1)
    row = lax.broadcasted_iota(jnp.int32, (PANEL, 2 * size), 0)
    below = lax.broadcasted_iota(jnp.int32, (PANEL, 1), 0)
    panel = work[start : start + PANEL, :]
    for j in range(PANEL):
        column = start + j
        factor = panel[:, column : column + 1] / panel[j : j + 1, column : column + 1]
        factor = jnp.where(below > j, factor, 0.0)
        panel = panel - factor * panel[j : j + 1, :]
    pivots = jnp.sum(jnp.where(lane == row + start, panel, 0.0), axis=1, keepdims=True)
    panel = panel / jnp.sqrt(pivots)
    out[start : start + PANEL, :] = panel[:, size:]
    if start + PANEL < size:
        outer = lax.dot_general(
            panel[:, :size],
            panel,
            (((0,), (0,)), ((), ())),
            precision=HIGHEST,
            preferred_element_type=jnp.float32,
        )
        work[start + PANEL :, :] = work[start + PANEL :, :] - outer[start + PANEL :, :]


def factors_kernel(
    scale, gradient, momentum, basis,
    hi, lo, ortho_hi, ortho_lo, lowrank, update_hi, update_lo, basis_t,
    stage_g, stage_m, other, pairs, part, left, halves, z_in, z_across, left_t,
    right, y_in, rz_in, rz_across, final, gathered, gram, gram_in, gram_peer, work, factor, factor_t,
    norm_own, norm_in,
    load_sem, feed_sem, pass_sem, rs_sem, z_sem, ag_sem, y_sem, rz_sem, yg_sem, gram_sem, norm_sem,
):
    rows, cols = hi.shape
    rank_local = basis.shape[1]
    slab = rows // SLABS
    feed = slab // 2
    loads = rows // feed
    chunks = cols // WIDTH
    f = lax.axis_index("fsdp")
    t = lax.axis_index("tensor")
    line = Line()
    half, depth = line.half, line.depth
    bits = bits_of("tensor")
    levels = len(bits)
    peer_y = {"fsdp": 1 - f}
    peer_z = {"replica": line.me + 1 - 2 * (line.me % 2)}
    upper = [(t // bit) % 2 for bit in bits]
    peers = [{"tensor": t + bit - 2 * bit * up} for bit, up in zip(bits, upper)]
    sizes = [slab // 2**i for i in range(levels + 1)]
    offs = [0]
    for i in range(levels):
        offs.append(offs[i] + upper[i] * sizes[i + 1])
    total = 2 * SLABS

    barrier = pltpu.get_barrier_semaphore()

    def greet(device):
        pl.semaphore_signal(barrier, inc=1, device_id=device, device_id_type=MESH)

    for device in [peer_y, line.inward] + peers:
        greet(device)
    if half > 1:
        @pl.when(depth > 0)
        def _():
            greet(line.outward)
    if half > 1:
        @pl.when(depth > 0)
        def _():
            pl.semaphore_wait(barrier, 3 + levels)

        @pl.when(depth == 0)
        def _():
            pl.semaphore_wait(barrier, 2 + levels)
    else:
        pl.semaphore_wait(barrier, 2 + levels)

    def load(i, slot):
        at = rows_of(i * feed, feed)
        return (
            pltpu.make_async_copy(gradient.at[0, at], stage_g.at[slot], load_sem.at[0, slot]),
            pltpu.make_async_copy(momentum.at[0, at], stage_m.at[slot], load_sem.at[1, slot]),
        )

    for i in range(2):
        for copy in load(i, i):
            copy.start()

    feeds = FEEDS // 2
    size = cols // FEEDS
    parity = line.me % 2

    def feed_copy(j):
        at = rows_of((parity * feeds + j) * size, size)
        return remote(basis.at[at], other.at[at], feed_sem.at[0, j], feed_sem.at[1, j], peer_y)

    def pass_copy(j, mine=True):
        at = rows_of(((parity if mine else 1 - parity) * feeds + j) * size, size)
        return remote(other.at[at], other.at[at], pass_sem.at[0, j], pass_sem.at[1, j], peer_z)

    for j in range(feeds):
        feed_copy(j).start()

    right[...] = jnp.zeros_like(right)

    def prepare(src, which):
        def body(i, carry):
            at = rows_of(i * 256, 256)
            high, low = split(src[at])
            pairs[which, at, :rank_local] = high
            pairs[which, at, rank_local:] = low
            return carry
        lax.fori_loop(0, cols // 256, body, 0)

    prepare(basis, 0)

    def place(q):
        return (f + q // SLABS) % 2, (q % SLABS) * slab

    def own(q, level):
        return part.at[q, rows_of(offs[level], sizes[level])]

    def rs_copy(q, i):
        away = offs[i] + (1 - upper[i]) * sizes[i + 1]
        return remote(
            part.at[q, rows_of(away, sizes[i + 1])], halves[i].at[q],
            rs_sem.at[0, i, q], rs_sem.at[1, i, q], peers[i],
        )

    def up_copy(q):
        return remote(own(q, levels), z_in.at[q], z_sem.at[0, 0, q], z_sem.at[1, 0, q], line.inward)

    def across_copy(q):
        return remote(own(q, levels), z_across.at[q], z_sem.at[0, 1, q], z_sem.at[1, 1, q], line.inward)

    def block(q, level, mine=True):
        blk, base = place(q)
        if mine:
            return left.at[blk, rows_of(base + offs[level], sizes[level])]
        at = offs[level - 1] + (1 - upper[level - 1]) * sizes[level]
        return left.at[blk, rows_of(base + at, sizes[level])]

    def back_copy(q):
        return remote(block(q, levels), block(q, levels), z_sem.at[0, 2, q], z_sem.at[1, 2, q], line.outward)

    def ag_copy(q, i, mine=True):
        ref = block(q, i + 1, mine)
        return remote(ref, ref, ag_sem.at[0, i, q], ag_sem.at[1, i, q], peers[i])

    def load_slab(q):
        for sub in range(2):
            i = q * 2 + sub
            for copy in load(i, sub):
                copy.wait()

            def body(b, carry):
                at = rows_of(b * 32, 32)
                high, low = split(stage_m[sub, at] + stage_g[sub, at].astype(jnp.float32))
                to = rows_of(i * feed + b * 32, 32, 16)
                hi[to] = high
                lo[to] = low
                return carry
            lax.fori_loop(0, feed // 32, body, 0)

            @pl.when(i + 2 < loads)
            def _():
                for copy in load(i + 2, sub):
                    copy.start()

    def left_part(q):
        which = q // SLABS
        base = (q % SLABS) * slab

        def body(b, carry):
            at = rows_of(base + b * 256, 256, 16)
            both = dot(hi[at], pairs[which])
            cross = dot(lo[at], pairs[which, :, :rank_local])
            part[q, rows_of(b * 256, 256)] = both[:, :rank_local] + both[:, rank_local:] + cross
            return carry
        lax.fori_loop(0, slab // 256, body, 0)
        rs_copy(q, 0).start()

    def right_part(q):
        blk, base = place(q)
        at = rows_of(base, slab, 16)
        flipped = left[blk, rows_of(base, slab)].T
        left_t[blk, :, pl.ds(pl.multiple_of(base, slab), slab)] = flipped
        high, low = split(flipped)
        stacked = jnp.concatenate([high, low], axis=0)

        def body(c, carry):
            lanes = pl.ds(pl.multiple_of(c * WIDTH, WIDTH), WIDTH)
            both = dot(stacked, hi[at, lanes])
            cross = dot(high, lo[at, lanes])
            right[q // SLABS, c] += both[:rank_local] + both[rank_local:] + cross
            return carry
        lax.fori_loop(0, chunks, body, 0)

    done = 2 * levels + 2 * half - 1

    def advance(q, s):
        if 1 <= s <= levels:
            rs_copy(q, s - 1).wait_recv()
            ref = own(q, s)
            ref[...] += halves[s - 1][q]
            if s < levels:
                rs_copy(q, s).start()
        u = s - levels
        if 0 <= u < half:
            @pl.when(depth == u)
            def _():
                if u > 0:
                    up_copy(q).wait_recv()
                    ref = own(q, levels)
                    ref[...] += z_in[q]
                if u < half - 1:
                    up_copy(q).start()
                else:
                    across_copy(q).start()
        v = u - half
        if 0 <= v < half:
            @pl.when(depth == half - 1 - v)
            def _():
                if v == 0:
                    across_copy(q).wait_recv()
                    block(q, levels)[...] = own(q, levels)[...] + z_across[q]
                else:
                    back_copy(q).wait_recv()
                if v < half - 1:
                    back_copy(q).start()
                ag_copy(q, levels - 1).start()
        w = s - (done - levels)
        if 1 <= w <= levels:
            i = levels - w
            ag_copy(q, i, False).wait_recv()
            if i > 0:
                ag_copy(q, i - 1).start()

    def y_copy(c):
        return remote(right.at[0, c], y_in.at[c], y_sem.at[0, c], y_sem.at[1, c], peer_y)

    early = chunks // 2

    def tick(n, carry):
        for s in range(done, 0, -1):
            for j, start in ((0, 0), (1, SLABS + GAP)):
                @pl.when((n - s >= start) & (n - s < start + SLABS))
                def _():
                    advance(n - s - start + j * SLABS, s)

        @pl.when((n >= 1) & (n <= feeds))
        def _():
            feed_copy(n - 1).wait_recv()
            pass_copy(n - 1).start()

        @pl.when(n < SLABS)
        def _():
            load_slab(n)

        @pl.when(n == SLABS + GAP)
        def _():
            for j in range(feeds):
                pass_copy(j, False).wait_recv()
            prepare(other, 1)

        for j, start in ((0, 0), (1, SLABS + GAP)):
            @pl.when((n >= start) & (n < start + SLABS))
            def _():
                left_part(n - start + j * SLABS)

        for j, start in ((0, 0), (1, SLABS + GAP)):
            @pl.when((n - done >= start) & (n - done < start + SLABS))
            def _():
                right_part(n - done - start + j * SLABS)

        @pl.when(n == done + SLABS - 1)
        def _():
            for c in range(early):
                y_copy(c).start()
        return carry

    lax.fori_loop(0, 2 * SLABS + GAP + done, tick, 0)

    rank = 2 * rank_local

    def gram_body(i, carry):
        lanes = pl.ds(pl.multiple_of(i * slab, slab), slab)
        for a in range(2):
            for b in range(2):
                gram[a * rank_local : (a + 1) * rank_local, b * rank_local : (b + 1) * rank_local] += dot(
                    left_t[a, :, lanes], left[b, rows_of(i * slab, slab)], HIGHEST
                )
        return carry

    gram[...] = jnp.zeros_like(gram)
    lax.fori_loop(0, SLABS, gram_body, 0)
    mine = rows_of(upper[0] * rank_local, rank_local)
    theirs = rows_of((1 - upper[0]) * rank_local, rank_local)
    gram_y = remote(gram.at[mine], gram_in, gram_sem.at[0, 0], gram_sem.at[1, 0], peer_y)
    gram_y.start()
    for c in range(early, chunks):
        y_copy(c).start()

    def rup_copy(c):
        return remote(right.at[1, c], rz_in.at[c], rz_sem.at[0, 0, c], rz_sem.at[1, 0, c], line.inward)

    def racross_copy(c):
        return remote(right.at[1, c], rz_across.at[c], rz_sem.at[0, 1, c], rz_sem.at[1, 1, c], line.inward)

    def rback_copy(c):
        return remote(final.at[c], final.at[c], rz_sem.at[0, 2, c], rz_sem.at[1, 2, c], line.outward)

    def yg_copy(c):
        return remote(final.at[c], gathered.at[c], yg_sem.at[0, c], yg_sem.at[1, c], peer_y)

    def radvance(c, s):
        if s == 0:
            y_copy(c).wait_recv()
            right[1, c] += y_in[c]
        if s < half:
            @pl.when(depth == s)
            def _():
                if s > 0:
                    rup_copy(c).wait_recv()
                    right[1, c] += rz_in[c]
                if s < half - 1:
                    rup_copy(c).start()
                else:
                    racross_copy(c).start()
        v = s - half
        if 0 <= v < half:
            @pl.when(depth == half - 1 - v)
            def _():
                if v == 0:
                    racross_copy(c).wait_recv()
                    final[c] = right[1, c] + rz_across[c]
                else:
                    rback_copy(c).wait_recv()
                if v < half - 1:
                    rback_copy(c).start()
                yg_copy(c).start()

    steps = chunks + 2 * half - 1
    panels = rank // PANEL
    ready = 2
    gram_x = remote(gram.at[mine], gram_peer, gram_sem.at[0, 1], gram_sem.at[1, 1], peers[0])
    made = 0
    for n in range(steps):
        for s in range(2 * half - 1, -1, -1):
            if 0 <= n - s < chunks:
                radvance(n - s, s)
        if n == 0:
            gram_y.wait()
            gram[mine] += gram_in[...]
            gram_x.start()
            gram_x.wait()
            work[mine, :rank] = gram[mine]
            work[theirs, :rank] = gram_peer[...]
            at = lax.broadcasted_iota(jnp.int32, (rank, rank), 0)
            to = lax.broadcasted_iota(jnp.int32, (rank, rank), 1)
            work[:, rank:] = jnp.where(at == to, 1.0, 0.0).astype(jnp.float32)
        goal = panels * (n + 1) // steps
        while made < goal:
            panel_step(work, factor, made * PANEL)
            made += 1

    factor_t[...] = factor[...].T

    def ortho_body(i, carry):
        at = rows_of(i * 256, 256, 16)
        value = dot(left[0, at], factor_t[:rank_local], HIGHEST) + dot(left[1, at], factor_t[rank_local:], HIGHEST)
        high, low = split(value)
        ortho_hi[at] = high
        ortho_lo[at] = low
        return carry
    lax.fori_loop(0, rows // 256, ortho_body, 0)

    norm_own[...] = jnp.zeros_like(norm_own)

    def final_body(c, carry):
        yg_copy(c).wait_recv()
        first = jnp.where(f == 0, gathered[c], final[c])
        second = jnp.where(f == 0, final[c], gathered[c])
        value = dot(factor[:, :rank_local], first, HIGHEST) + dot(factor[:, rank_local:], second, HIGHEST)
        value = value * (1.0 / line.n)
        basis_t[:, pl.ds(pl.multiple_of(c * WIDTH, WIDTH), WIDTH)] = value
        square = value * value
        flat = square[:, :128]
        for k in range(1, WIDTH // 128):
            flat = flat + square[:, k * 128 : (k + 1) * 128]
        norm_own[...] += jnp.sum(flat.T, axis=0, keepdims=True)
        return carry
    lax.fori_loop(0, chunks, final_body, 0)

    for i in range(levels):
        src = norm_own if i == 0 else norm_in.at[levels + i]
        copy = remote(src, norm_in.at[i], norm_sem.at[0, i], norm_sem.at[1, i], peers[i])
        copy.start()
        copy.wait()
        norm_in[levels + i + 1] = src[...] + norm_in[i]
    total_row = norm_in[2 * levels][0:1, :]
    squares = jnp.broadcast_to(total_row, (128, rank)).T
    norms = jnp.sqrt(squares + 1e-12)
    norms = jnp.concatenate([norms] * (WIDTH // 128), axis=1)

    def out_body(c, carry):
        lanes = pl.ds(pl.multiple_of(c * WIDTH, WIDTH), WIDTH)
        value = basis_t[:, lanes]
        lowrank[:, lanes] = (0.05 * value).astype(jnp.bfloat16)
        value = value / norms
        basis_t[:, lanes] = value
        high, low = split(scale * value)
        update_hi[:, lanes] = high
        update_lo[:, lanes] = low
        return carry
    lax.fori_loop(0, chunks, out_body, 0)

    for j in range(feeds):
        feed_copy(j).wait_send()
        pass_copy(j).wait_send()

    def drain(q, carry):
        for i in range(levels):
            rs_copy(q, i).wait_send()
            ag_copy(q, i).wait_send()

        @pl.when(depth < half - 1)
        def _():
            up_copy(q).wait_send()

        @pl.when(depth == half - 1)
        def _():
            across_copy(q).wait_send()

        @pl.when(depth > 0)
        def _():
            back_copy(q).wait_send()
        return carry
    lax.fori_loop(0, total, drain, 0)

    def rdrain(c, carry):
        y_copy(c).wait_send()
        yg_copy(c).wait_send()

        @pl.when(depth < half - 1)
        def _():
            rup_copy(c).wait_send()

        @pl.when(depth == half - 1)
        def _():
            racross_copy(c).wait_send()

        @pl.when(depth > 0)
        def _():
            rback_copy(c).wait_send()
        return carry
    lax.fori_loop(0, chunks, rdrain, 0)


def outputs_kernel(hi, lo, ortho_hi, ortho_lo, lowrank, update_hi, update_lo, basis_t, update, momentum_new, basis_new):
    i = pl.program_id(0)
    tile, cols = update.shape
    rank_local = basis_new.shape[1]
    at = rows_of(i * tile, tile, 16)

    def body(c, carry):
        lanes = pl.ds(pl.multiple_of(c * WIDTH, WIDTH), WIDTH)
        high = ortho_hi[at]
        buffer = hi[at, lanes].astype(jnp.float32) + lo[at, lanes].astype(jnp.float32)
        momentum_new[0, :, lanes] = buffer - dot(high, lowrank[:, lanes])
        top = update_hi[:, lanes]
        value = dot(high, top) + dot(high, update_lo[:, lanes]) + dot(ortho_lo[at], top)
        update[:, lanes] = value.astype(jnp.bfloat16)
        return carry
    lax.fori_loop(0, cols // WIDTH, body, 0)
    width = basis_new.shape[0]
    start = rows_of(lax.axis_index("fsdp") * rank_local, rank_local)
    basis_new[...] = basis_t[start, pl.ds(pl.multiple_of(i * width, 128), width)].T


def fast_local(gradient, momentum, basis):
    rows, cols = gradient.shape[1:]
    rank_local = basis.shape[1]
    rank = 2 * rank_local
    levels = len(bits_of("tensor"))
    total = 2 * SLABS
    slab = rows // SLABS
    feed = slab // 2
    chunks = cols // WIDTH
    scale = (rows * 2 * cols * lax.axis_size("tensor") / rank) ** 0.5
    f32, bf16 = jnp.float32, jnp.bfloat16
    small = slab // 2**levels
    vmem = pl.BlockSpec(memory_space=VMEM)
    outs = [
        ((rows, cols), bf16), ((rows, cols), bf16), ((rows, rank), bf16), ((rows, rank), bf16),
        ((rank, cols), bf16), ((rank, cols), bf16), ((rank, cols), bf16), ((rank, cols), f32),
    ]
    dma = pltpu.SemaphoreType.DMA
    wide = (chunks, rank_local, WIDTH)
    made = pl.pallas_call(
        functools.partial(factors_kernel, scale),
        out_shape=tuple(VMEM(shape, kind) for shape, kind in outs),
        in_specs=[pl.BlockSpec(memory_space=ANY), pl.BlockSpec(memory_space=ANY), vmem],
        out_specs=tuple(vmem for _ in outs),
        scratch_shapes=[
            VMEM((2, feed, cols), bf16), VMEM((2, feed, cols), f32),
            VMEM((cols, rank_local), f32), VMEM((2, cols, rank), bf16),
            VMEM((total, slab, rank_local), f32), VMEM((2, rows, rank_local), f32),
            [VMEM((total, slab // 2 ** (i + 1), rank_local), f32) for i in range(levels)],
            VMEM((total, small, rank_local), f32), VMEM((total, small, rank_local), f32),
            VMEM((2, rank_local, rows), f32),
            VMEM((2,) + wide, f32), VMEM(wide, f32), VMEM(wide, f32), VMEM(wide, f32), VMEM(wide, f32), VMEM(wide, f32),
            VMEM((rank, rank), f32), VMEM((rank_local, rank), f32), VMEM((rank_local, rank), f32),
            VMEM((rank, 2 * rank), f32),
            VMEM((rank, rank), f32), VMEM((rank, rank), f32),
            VMEM((8, rank), f32), VMEM((2 * levels + 1, 8, rank), f32),
            dma((2, 2)), dma((2, FEEDS // 2)), dma((2, FEEDS // 2)), dma((2, levels, total)), dma((2, 3, total)),
            dma((2, levels, total)), dma((2, chunks)), dma((2, 3, chunks)), dma((2, chunks)), dma((2, 2)), dma((2, levels)),
        ],
        compiler_params=pltpu.CompilerParams(collective_id=0, has_side_effects=True, vmem_limit_bytes=36 << 20),
    )(gradient, momentum, basis)
    tile = slab
    return pl.pallas_call(
        outputs_kernel,
        grid=(rows // tile,),
        out_shape=(
            jax.ShapeDtypeStruct((rows, cols), bf16),
            jax.ShapeDtypeStruct((1, rows, cols), f32),
            jax.ShapeDtypeStruct((cols, rank_local), f32),
        ),
        in_specs=[vmem] * len(outs),
        out_specs=(
            pl.BlockSpec((tile, cols), lambda i: (i, 0)),
            pl.BlockSpec((1, tile, cols), lambda i: (0, i, 0)),
            pl.BlockSpec((cols * tile // rows, rank_local), lambda i: (i, 0)),
        ),
        compiler_params=pltpu.CompilerParams(vmem_limit_bytes=18 << 20),
    )(*made)


def fits(mesh):
    shape = mesh.shape
    tensor, replica = shape["tensor"], shape["replica"]
    return shape["fsdp"] == 2 and tensor > 1 and tensor & (tensor - 1) == 0 and replica % 2 == 0


def solution(mesh):
    return jax.shard_map(
        fast_local if fits(mesh) else local,
        mesh=mesh,
        in_specs=(
            P("replica", "fsdp", "tensor"),
            P("replica", "fsdp", "tensor"),
            P("tensor", "fsdp"),
        ),
        out_specs=(P("fsdp", "tensor"), P("replica", "fsdp", "tensor"), P("tensor", "fsdp")),
        check_vma=False,
    )
```

```python
import functools

import jax
import jax.numpy as jnp
from jax import lax
from jax.experimental import pallas as pl
from jax.experimental.pallas import tpu as pltpu
from jax.sharding import PartitionSpec as P

HIGHEST = lax.Precision.HIGHEST
HIGH = lax.Precision.HIGH
BLOCK = 16


def mm(a, b, precision):
    return jnp.dot(a, b, precision=precision, preferred_element_type=jnp.float32)


def pick(parts, index):
    return lax.dynamic_index_in_dim(parts, index, 0, keepdims=False)


def shift(x, axis, step):
    n = lax.axis_size(axis)
    return lax.ppermute(x, axis, [(i, (i + step) % n) for i in range(n)])


def swap(x, axis, bit):
    n = lax.axis_size(axis)
    return lax.ppermute(x, axis, [(i, i ^ bit) for i in range(n)])


def bits_of(axis):
    n = lax.axis_size(axis)
    bits, bit = [], 1
    while bit < n:
        bits.append(bit)
        bit *= 2
    return bits


def halve(x, axis, bits):
    for bit in bits:
        upper = (lax.axis_index(axis) // bit) % 2
        parts = x.reshape(2, x.shape[0] // 2, x.shape[1])
        x = pick(parts, upper) + swap(pick(parts, 1 - upper), axis, bit)
    return x


def double(x, axis, bits):
    for bit in reversed(bits):
        upper = (lax.axis_index(axis) // bit) % 2 == 1
        other = swap(x, axis, bit)
        x = jnp.concatenate([jnp.where(upper, other, x), jnp.where(upper, x, other)], axis=0)
    return x


def ring_scatter(x, axis):
    n = lax.axis_size(axis)
    me = lax.axis_index(axis)
    parts = x.reshape(n, 2, x.shape[0] // (2 * n), x.shape[1])
    up, down = parts[:, 0], parts[:, 1]
    a, b = pick(up, (me + n - 1) % n), pick(down, (me + 1) % n)
    for step in range(n - 1):
        a = shift(a, axis, 1) + pick(up, (me + 2 * n - step - 2) % n)
        b = shift(b, axis, n - 1) + pick(down, (me + step + 2) % n)
    return jnp.concatenate([a, b], axis=0)


def ring_gather(x, axis):
    n = lax.axis_size(axis)
    me = lax.axis_index(axis)
    half = x.shape[0] // 2
    a, b = x[:half], x[half:]
    out = jnp.zeros((n, 2, half, x.shape[1]), x.dtype)

    def put(out, value, chunk, side):
        return lax.dynamic_update_slice(out, value[None, None], (chunk, side, 0, 0))

    out = put(put(out, a, me, 0), b, me, 1)
    for step in range(n - 1):
        a = shift(a, axis, 1)
        b = shift(b, axis, n - 1)
        out = put(out, a, (me + n - step - 1) % n, 0)
        out = put(out, b, (me + step + 1) % n, 1)
    return out.reshape(n * x.shape[0], x.shape[1])


def sum_over(x, axis, bits, ring):
    half = x.shape[0] // 2
    first = ring_scatter(halve(x[:half], axis, bits), ring)
    second = halve(ring_scatter(x[half:], ring), axis, bits)
    first = double(ring_gather(first, ring), axis, bits)
    second = ring_gather(double(second, axis, bits), ring)
    return jnp.concatenate([first, second], axis=0)


def invert_kernel(gram_ref, out_ref, work):
    size = gram_ref.shape[0]
    rows = lax.broadcasted_iota(jnp.int32, (size, size), 0)
    cols = lax.broadcasted_iota(jnp.int32, (size, size), 1)
    work[:, :size] = gram_ref[...]
    work[:, size:] = jnp.where(rows == cols, 1.0, 0.0).astype(jnp.float32)
    lane = lax.broadcasted_iota(jnp.int32, (BLOCK, 2 * size), 1)
    row = lax.broadcasted_iota(jnp.int32, (BLOCK, 2 * size), 0)
    below = lax.broadcasted_iota(jnp.int32, (BLOCK, 1), 0)
    for start in range(0, size, BLOCK):
        panel = work[start : start + BLOCK, :]
        for j in range(BLOCK):
            column = start + j
            factor = panel[:, column : column + 1] / panel[j : j + 1, column : column + 1]
            factor = jnp.where(below > j, factor, 0.0)
            panel = panel - factor * panel[j : j + 1, :]
        pivots = jnp.sum(jnp.where(lane == row + start, panel, 0.0), axis=1, keepdims=True)
        panel = panel / jnp.sqrt(pivots)
        out_ref[start : start + BLOCK, :] = panel[:, size:]
        if start + BLOCK < size:
            outer = lax.dot_general(
                panel[:, :size],
                panel,
                (((0,), (0,)), ((), ())),
                precision=HIGHEST,
                preferred_element_type=jnp.float32,
            )
            work[start + BLOCK :, :] = work[start + BLOCK :, :] - outer[start + BLOCK :, :]


def inverse_factor(gram, interpret=False):
    size = gram.shape[0]
    return pl.pallas_call(
        invert_kernel,
        out_shape=jax.ShapeDtypeStruct((size, size), jnp.float32),
        in_specs=[pl.BlockSpec(memory_space=pltpu.VMEM)],
        out_specs=pl.BlockSpec(memory_space=pltpu.VMEM),
        scratch_shapes=[pltpu.VMEM((size, 2 * size), jnp.float32)],
        interpret=interpret,
    )(gram)


def gather_columns(x, axis):
    for bit in bits_of(axis):
        upper = (lax.axis_index(axis) // bit) % 2 == 1
        other = swap(x, axis, bit)
        x = jnp.concatenate([jnp.where(upper, other, x), jnp.where(upper, x, other)], axis=1)
    return x


def local(gradient, momentum, basis):
    replicas = lax.axis_size("replica")
    rank_local = basis.shape[1]
    rank = rank_local * lax.axis_size("fsdp")
    rows = gradient.shape[1] * lax.axis_size("fsdp")
    columns = gradient.shape[2] * lax.axis_size("tensor")
    buffer = momentum[0] + gradient[0].astype(jnp.float32)

    left = mm(buffer, gather_columns(basis, "fsdp"), HIGH)
    bits = bits_of("tensor")
    left = halve(left, "tensor", bits[:1])
    left = sum_over(left, "tensor", bits[1:], "replica")
    left = double(left, "tensor", bits[:1]) / replicas

    gram = mm(left.T, left, HIGHEST)
    for bit in bits_of("fsdp"):
        gram = gram + swap(gram, "fsdp", bit)
    ortho = mm(left, inverse_factor(gram).T, HIGHEST)

    right = mm(buffer.T, ortho, HIGH)
    right = sum_over(right, "fsdp", bits_of("fsdp"), "replica") / replicas
    squares = jnp.sum(right * right, axis=0, keepdims=True)
    for bit in bits_of("tensor"):
        squares = squares + swap(squares, "tensor", bit)
    norms = jnp.sqrt(squares + 1e-12)
    basis_full = right / norms
    lowrank = mm(ortho, right.T, lax.Precision.DEFAULT)
    momentum_new = (buffer - 0.05 * lowrank)[None]
    scale = (rows * columns / rank) ** 0.5
    update = (scale * mm(ortho, basis_full.T, HIGH)).astype(jnp.bfloat16)
    offset = lax.axis_index("fsdp") * rank_local
    basis_new = lax.dynamic_slice_in_dim(basis_full, offset, rank_local, 1)
    return (update, momentum_new, basis_new)

MESH = pl.DeviceIdType.MESH
SLABS = 8
PAIR = 2
FEEDS = 8
CHUNK = 128
WIDTH = 256
EVERY = 2
SECOND = 25
NEAR = 2
FAR = 5
HOP = 3
FEED = 5
MEET = 4
RATE = 2
PANEL = 16
VMEM = pltpu.VMEM
ANY = pl.ANY


def dot(a, b, precision=None):
    return jnp.dot(a, b, precision=precision, preferred_element_type=jnp.float32)


def split(x):
    high = x.astype(jnp.bfloat16)
    return high, (x - high.astype(jnp.float32)).astype(jnp.bfloat16)


def rows_of(start, size, unit=8):
    return pl.ds(pl.multiple_of(start, unit), size)


class Line:
    def __init__(self):
        self.n = lax.axis_size("replica")
        self.half = self.n // 2
        me = lax.axis_index("replica")
        low = me < self.half
        self.me = me
        self.depth = jnp.where(low, me, self.n - 1 - me)
        self.inward = {"replica": jnp.where(low, me + 1, me - 1)}
        outward = jnp.where(low, me - 1, me + 1)
        self.outward = {"replica": jnp.where(self.depth > 0, outward, self.inward["replica"])}


def remote(src, dst, send, recv, device):
    return pltpu.make_async_remote_copy(
        src_ref=src, dst_ref=dst, send_sem=send, recv_sem=recv, device_id=device, device_id_type=MESH
    )


def outer(a, b):
    return lax.dot_general(
        a, b, (((0,), (0,)), ((), ())), precision=HIGHEST, preferred_element_type=jnp.float32
    )


def eliminate(panel, start):
    size = panel.shape[1] // 2
    lanes = 128
    columns = [jnp.broadcast_to(panel[:, start + c : start + c + 1], (PANEL, lanes)) for c in range(PANEL)]
    tiles = [panel[:, k : k + lanes] for k in range(0, 2 * size, lanes)]
    live = [k for k in range(len(tiles)) if start < (k + 1) * lanes and k * lanes < size + start + PANEL]
    below = lax.broadcasted_iota(jnp.int32, (PANEL, lanes), 0)
    pivots = jnp.zeros((PANEL, lanes), jnp.float32)
    for j in range(PANEL):
        pivot = jnp.broadcast_to(columns[j][j : j + 1, :], (PANEL, lanes))
        pivots = jnp.where(below == j, pivot, pivots)
        factor = jnp.where(below > j, columns[j] * (1.0 / pivot), 0.0)
        for c in range(j + 1, PANEL):
            columns[c] = columns[c] - factor * columns[c][j : j + 1, :]
        for k in live:
            tiles[k] = tiles[k] - factor * tiles[k][j : j + 1, :]
    root = 1.0 / jnp.sqrt(pivots)
    for k in live:
        tiles[k] = tiles[k] * root
    return jnp.concatenate(tiles, axis=1)


def panel_step(work, out, start):
    size = out.shape[0]
    panel = eliminate(work[start : start + PANEL, :], start)
    out[start : start + PANEL, :] = panel[:, size:]
    after = start + PANEL
    if after < size:
        work[after : after + PANEL, :] = work[after : after + PANEL, :] - outer(panel[:, after : after + PANEL], panel)
        after += PANEL
    if after < size:
        low = after // 128 * 128
        high = size + (start + PANEL + 127) // 128 * 128
        change = outer(panel[:, low:size], panel[:, low:high])
        work[after:, low:high] = work[after:, low:high] - change[after - low :, :]


def factors_kernel(
    scale, gradient, momentum, basis,
    hi, lo, ortho_hi, ortho_lo, lowrank, update_hi, update_lo, basis_t,
    stage_g, stage_m, other, pairs, part, left, halves, z_in, z_across, left_t,
    right, y_in, rz_in, rz_across, final, gathered, gram, gram_in, gram_peer, work, factor, factor_hi, factor_lo,
    norm_own, norm_in,
    load_sem, feed_sem, pass_sem, rs_sem, z_sem, ag_sem, y_sem, rz_sem, yg_sem, gram_sem, norm_sem,
):
    rows, cols = hi.shape
    rank_local = basis.shape[1]
    slab = rows // SLABS
    chunks = cols // CHUNK
    f = lax.axis_index("fsdp")
    t = lax.axis_index("tensor")
    line = Line()
    half, depth = line.half, line.depth
    bits = bits_of("tensor")
    levels = len(bits)
    peer_y = {"fsdp": 1 - f}
    peer_z = {"replica": line.me + 1 - 2 * (line.me % 2)}
    upper = [(t // bit) % 2 for bit in bits]
    peers = [{"tensor": t + bit - 2 * bit * up} for bit, up in zip(bits, upper)]
    sizes = [slab // 2**i for i in range(levels + 1)]
    offs = [0]
    for i in range(levels):
        offs.append(offs[i] + upper[i] * sizes[i + 1])
    total = 2 * SLABS

    barrier = pltpu.get_barrier_semaphore()

    def greet(device):
        pl.semaphore_signal(barrier, inc=1, device_id=device, device_id_type=MESH)

    for device in [peer_y, line.inward] + peers:
        greet(device)
    if half > 1:
        @pl.when(depth > 0)
        def _():
            greet(line.outward)
    if half > 1:
        @pl.when(depth > 0)
        def _():
            pl.semaphore_wait(barrier, 3 + levels)

        @pl.when(depth == 0)
        def _():
            pl.semaphore_wait(barrier, 2 + levels)
    else:
        pl.semaphore_wait(barrier, 2 + levels)

    def load(i, slot):
        at = rows_of(i * slab, slab)
        return (
            pltpu.make_async_copy(gradient.at[0, at], stage_g.at[slot], load_sem.at[0, slot]),
            pltpu.make_async_copy(momentum.at[0, at], stage_m.at[slot], load_sem.at[1, slot]),
        )

    for i in range(2):
        for copy in load(i, i):
            copy.start()

    feeds = FEEDS // 2
    size = cols // FEEDS
    parity = line.me % 2

    def feed_copy(j):
        at = rows_of((parity * feeds + j) * size, size)
        return remote(basis.at[at], other.at[at], feed_sem.at[0, j], feed_sem.at[1, j], peer_y)

    def pass_copy(j, mine=True):
        at = rows_of(((parity if mine else 1 - parity) * feeds + j) * size, size)
        return remote(other.at[at], other.at[at], pass_sem.at[0, j], pass_sem.at[1, j], peer_z)

    for j in range(feeds):
        feed_copy(j).start()

    right[...] = jnp.zeros_like(right)

    def prepare(src, which):
        def body(i, carry):
            at = rows_of(i * 256, 256)
            high, low = split(src[at])
            pairs[which, at, :rank_local] = high
            pairs[which, at, rank_local:] = low
            return carry
        lax.fori_loop(0, cols // 256, body, 0)

    prepare(basis, 0)

    def place(q):
        return (f + q // SLABS) % 2, (q % SLABS) * slab

    def own(q, level):
        return part.at[q, rows_of(offs[level], sizes[level])]

    def rs_copy(q, i):
        away = offs[i] + (1 - upper[i]) * sizes[i + 1]
        return remote(
            part.at[q, rows_of(away, sizes[i + 1])], halves[i].at[q],
            rs_sem.at[0, i, q], rs_sem.at[1, i, q], peers[i],
        )

    def up_copy(q):
        return remote(own(q, levels), z_in.at[q], z_sem.at[0, 0, q], z_sem.at[1, 0, q], line.inward)

    def across_copy(q):
        return remote(own(q, levels), z_across.at[q], z_sem.at[0, 1, q], z_sem.at[1, 1, q], line.inward)

    def block(q, level, mine=True):
        blk, base = place(q)
        if mine:
            return left.at[blk, rows_of(base + offs[level], sizes[level])]
        at = offs[level - 1] + (1 - upper[level - 1]) * sizes[level]
        return left.at[blk, rows_of(base + at, sizes[level])]

    def back_copy(q):
        return remote(block(q, levels), block(q, levels), z_sem.at[0, 2, q], z_sem.at[1, 2, q], line.outward)

    def ag_copy(q, i, mine=True):
        ref = block(q, i + 1, mine)
        return remote(ref, ref, ag_sem.at[0, i, q], ag_sem.at[1, i, q], peers[i])

    def load_slab(q):
        slot = q % 2
        for copy in load(q, slot):
            copy.wait()

        def body(b, carry):
            at = rows_of(b * 32, 32)
            high, low = split(stage_m[slot, at] + stage_g[slot, at].astype(jnp.float32))
            to = rows_of(q * slab + b * 32, 32, 16)
            hi[to] = high
            lo[to] = low
            return carry
        lax.fori_loop(0, slab // 32, body, 0)

        @pl.when(q + 2 < SLABS)
        def _():
            for copy in load(q + 2, slot):
                copy.start()

    def left_part(q):
        which = q // SLABS
        at = rows_of((q % SLABS) * slab, slab, 16)
        both = dot(hi[at], pairs[which])
        cross = dot(lo[at], pairs[which, :, :rank_local])
        part[q] = both[:, :rank_local] + both[:, rank_local:] + cross
        rs_copy(q, 0).start()

    def right_part(q):
        blk, base = place(q - PAIR + 1)
        size = PAIR * slab
        at = rows_of(base, size, 16)
        flipped = left[blk, rows_of(base, size)].T
        left_t[blk, :, pl.ds(pl.multiple_of(base, size), size)] = flipped
        high, low = split(flipped)
        stacked = jnp.concatenate([high, low], axis=0)
        which = q // SLABS
        for c in range(cols // WIDTH):
            lanes = pl.ds(c * WIDTH, WIDTH)
            both = dot(stacked, hi[at, lanes])
            both = both[:rank_local] + both[rank_local:] + dot(high, lo[at, lanes])
            for k in range(WIDTH // CHUNK):
                right[which, c * (WIDTH // CHUNK) + k] += both[:, k * CHUNK : (k + 1) * CHUNK]

    done = 2 * levels + 2 * half - 1

    def advance(q, s):
        if 1 <= s <= levels:
            rs_copy(q, s - 1).wait_recv()
            ref = own(q, s)
            ref[...] += halves[s - 1][q]
            if s < levels:
                rs_copy(q, s).start()
        u = s - levels
        if 0 <= u < half:
            @pl.when(depth == u)
            def _():
                if u > 0:
                    up_copy(q).wait_recv()
                    ref = own(q, levels)
                    ref[...] += z_in[q]
                if u < half - 1:
                    up_copy(q).start()
                else:
                    across_copy(q).start()
        v = u - half
        if 0 <= v < half:
            @pl.when(depth == half - 1 - v)
            def _():
                if v == 0:
                    across_copy(q).wait_recv()
                    block(q, levels)[...] = own(q, levels)[...] + z_across[q]
                else:
                    back_copy(q).wait_recv()
                if v < half - 1:
                    back_copy(q).start()
                ag_copy(q, levels - 1).start()
        w = s - (done - levels)
        if 1 <= w <= levels:
            i = levels - w
            ag_copy(q, i, False).wait_recv()
            if i > 0:
                ag_copy(q, i - 1).start()

    def y_copy(c):
        return remote(right.at[0, c], y_in.at[c], y_sem.at[0, c], y_sem.at[1, c], peer_y)

    early = chunks * 3 // 4

    spans = [0, NEAR] + [FAR] * (levels - 1) + [FAR] * (2 * half - 1) + [FAR] * (levels - 1) + [NEAR]
    delay = [sum(spans[: s + 1]) for s in range(done + 1)]

    def window(n, s):
        local = n - delay[s]
        first = (local >= 0) & (local < EVERY * SLABS) & (local % EVERY == 0)
        second = (local >= SECOND) & (local < SECOND + SLABS)
        return first | second, jnp.where(local < SECOND, local // EVERY, local - SECOND + SLABS)

    def tick(n, carry):
        for s in range(done, 0, -1):
            active, q = window(n, s)

            @pl.when(active)
            def _():
                advance(q, s)

        @pl.when((n >= FEED) & (n < FEED + 2 * feeds) & ((n - FEED) % 2 == 0))
        def _():
            feed_copy((n - FEED) // 2).wait_recv()
            pass_copy((n - FEED) // 2).start()

        @pl.when((n < EVERY * SLABS) & (n % EVERY == 0))
        def _():
            load_slab(n // EVERY)

        @pl.when(n == SECOND)
        def _():
            for j in range(feeds):
                pass_copy(j, False).wait_recv()
            prepare(other, 1)

        active, q = window(n, 0)

        @pl.when(active)
        def _():
            left_part(q)

        active, q = window(n, done)

        @pl.when(active & (q % PAIR == PAIR - 1))
        def _():
            right_part(q)

        @pl.when(n == delay[done] + EVERY * (SLABS - 1))
        def _():
            for c in range(early):
                y_copy(c).start()
        return carry

    lax.fori_loop(0, SECOND + SLABS + delay[done], tick, 0)

    rank = 2 * rank_local

    span = PAIR * slab

    def gram_body(i, carry):
        lanes = pl.ds(pl.multiple_of(i * span, span), span)
        for a in range(2):
            for b in range(2):
                gram[a * rank_local : (a + 1) * rank_local, b * rank_local : (b + 1) * rank_local] += dot(
                    left_t[a, :, lanes], left[b, rows_of(i * span, span)], HIGHEST
                )
        return carry

    gram[...] = jnp.zeros_like(gram)
    lax.fori_loop(0, SLABS // PAIR, gram_body, 0)
    mine = rows_of(upper[0] * rank_local, rank_local)
    theirs = rows_of((1 - upper[0]) * rank_local, rank_local)
    gram_y = remote(gram.at[mine], gram_in, gram_sem.at[0, 0], gram_sem.at[1, 0], peer_y)
    gram_y.start()
    for c in range(early, chunks):
        y_copy(c).start()

    def rup_copy(c):
        return remote(right.at[1, c], rz_in.at[c], rz_sem.at[0, 0, c], rz_sem.at[1, 0, c], line.inward)

    def racross_copy(c):
        return remote(right.at[1, c], rz_across.at[c], rz_sem.at[0, 1, c], rz_sem.at[1, 1, c], line.inward)

    def rback_copy(c):
        return remote(final.at[c], final.at[c], rz_sem.at[0, 2, c], rz_sem.at[1, 2, c], line.outward)

    def yg_copy(c):
        return remote(final.at[c], gathered.at[c], yg_sem.at[0, c], yg_sem.at[1, c], peer_y)

    def radvance(c, s):
        if s == 0:
            y_copy(c).wait_recv()
            right[1, c] += y_in[c]
        if s < half:
            @pl.when(depth == s)
            def _():
                if s > 0:
                    rup_copy(c).wait_recv()
                    right[1, c] += rz_in[c]
                if s < half - 1:
                    rup_copy(c).start()
                else:
                    racross_copy(c).start()
        v = s - half
        if 0 <= v < half:
            @pl.when(depth == half - 1 - v)
            def _():
                if v == 0:
                    racross_copy(c).wait_recv()
                    final[c] = right[1, c] + rz_across[c]
                else:
                    rback_copy(c).wait_recv()
                if v < half - 1:
                    rback_copy(c).start()
                yg_copy(c).start()

    steps = chunks + HOP * (2 * half - 1)
    panels = rank // PANEL
    gram_x = remote(gram.at[mine], gram_peer, gram_sem.at[0, 1], gram_sem.at[1, 1], peers[0])
    def ortho_part(i):
        at = pl.ds(i * 256, 256)
        value = 0.0
        for a in range(2):
            high, low = split(left[a, at])
            b = pl.ds(a * rank_local, rank_local)
            top = factor_hi[b]
            both = jnp.concatenate([high, high, low], axis=1)
            value = value + dot(both, jnp.concatenate([top, factor_lo[b], top], axis=0))
        high, low = split(value)
        ortho_hi[at] = high
        ortho_lo[at] = low

    def flip_factor():
        high, low = split(factor[...].T)
        factor_hi[...] = high
        factor_lo[...] = low

    jobs = [functools.partial(panel_step, work, factor, p * PANEL) for p in range(panels)] + [flip_factor]
    jobs += [functools.partial(ortho_part, i) for i in range(rows // 256)]
    for n in range(steps):
        for s in range(2 * half - 1, -1, -1):
            if 0 <= n - HOP * s < chunks:
                radvance(n - HOP * s, s)
        if n == MEET:
            gram_y.wait()
            gram[mine] += gram_in[...]
            gram_x.start()
        if n == MEET + 1:
            gram_x.wait()
            work[mine, :rank] = gram[mine]
            work[theirs, :rank] = gram_peer[...]
            at = lax.broadcasted_iota(jnp.int32, (rank, rank), 0)
            to = lax.broadcasted_iota(jnp.int32, (rank, rank), 1)
            work[:, rank:] = jnp.where(at == to, 1.0, 0.0).astype(jnp.float32)
        if n > MEET:
            for job in jobs[:RATE]:
                job()
            jobs = jobs[RATE:]
    for job in jobs:
        job()

    norm_own[...] = jnp.zeros_like(norm_own)

    def final_body(c, carry):
        several = WIDTH // CHUNK
        first, second = [], []
        for k in range(several):
            i = c * several + k
            yg_copy(i).wait_recv()
            first.append(jnp.where(f == 0, gathered[i], final[i]))
            second.append(jnp.where(f == 0, final[i], gathered[i]))
        first, second = jnp.concatenate(first, axis=1), jnp.concatenate(second, axis=1)
        value = dot(factor[:, :rank_local], first, HIGHEST) + dot(factor[:, rank_local:], second, HIGHEST)
        value = value * (1.0 / line.n)
        basis_t[:, pl.ds(pl.multiple_of(c * WIDTH, WIDTH), WIDTH)] = value
        square = value * value
        flat = square[:, :128]
        for k in range(1, WIDTH // 128):
            flat = flat + square[:, k * 128 : (k + 1) * 128]
        norm_own[...] += jnp.sum(flat.T, axis=0, keepdims=True)
        return carry
    lax.fori_loop(0, cols // WIDTH, final_body, 0)

    for i in range(levels):
        src = norm_own if i == 0 else norm_in.at[levels + i]
        copy = remote(src, norm_in.at[i], norm_sem.at[0, i], norm_sem.at[1, i], peers[i])
        copy.start()
        copy.wait()
        norm_in[levels + i + 1] = src[...] + norm_in[i]
    total_row = norm_in[2 * levels][0:1, :]
    squares = jnp.broadcast_to(total_row, (128, rank)).T
    norms = jnp.sqrt(squares + 1e-12)
    norms = jnp.concatenate([norms] * (WIDTH // 128), axis=1)

    def out_body(c, carry):
        lanes = pl.ds(pl.multiple_of(c * WIDTH, WIDTH), WIDTH)
        value = basis_t[:, lanes]
        lowrank[:, lanes] = (0.05 * value).astype(jnp.bfloat16)
        value = value / norms
        basis_t[:, lanes] = value
        high, low = split(scale * value)
        update_hi[:, lanes] = high
        update_lo[:, lanes] = low
        return carry
    lax.fori_loop(0, cols // WIDTH, out_body, 0)

    for j in range(feeds):
        feed_copy(j).wait_send()
        pass_copy(j).wait_send()

    def drain(q, carry):
        for i in range(levels):
            rs_copy(q, i).wait_send()
            ag_copy(q, i).wait_send()

        @pl.when(depth < half - 1)
        def _():
            up_copy(q).wait_send()

        @pl.when(depth == half - 1)
        def _():
            across_copy(q).wait_send()

        @pl.when(depth > 0)
        def _():
            back_copy(q).wait_send()
        return carry
    lax.fori_loop(0, total, drain, 0)

    def rdrain(c, carry):
        y_copy(c).wait_send()
        yg_copy(c).wait_send()

        @pl.when(depth < half - 1)
        def _():
            rup_copy(c).wait_send()

        @pl.when(depth == half - 1)
        def _():
            racross_copy(c).wait_send()

        @pl.when(depth > 0)
        def _():
            rback_copy(c).wait_send()
        return carry
    lax.fori_loop(0, chunks, rdrain, 0)


def outputs_kernel(hi, lo, ortho_hi, ortho_lo, lowrank, update_hi, update_lo, basis_t, update, momentum_new, basis_new):
    i = pl.program_id(0)
    tile, cols = update.shape
    rank_local = basis_new.shape[1]
    at = rows_of(i * tile, tile, 16)

    def body(c, carry):
        lanes = pl.ds(pl.multiple_of(c * WIDTH, WIDTH), WIDTH)
        high = ortho_hi[at]
        buffer = hi[at, lanes].astype(jnp.float32) + lo[at, lanes].astype(jnp.float32)
        momentum_new[0, :, lanes] = buffer - dot(high, lowrank[:, lanes])
        top = update_hi[:, lanes]
        left = jnp.concatenate([high, high, ortho_lo[at]], axis=1)
        right = jnp.concatenate([top, update_lo[:, lanes], top], axis=0)
        update[:, lanes] = dot(left, right).astype(jnp.bfloat16)
        return carry
    lax.fori_loop(0, cols // WIDTH, body, 0, unroll=cols // WIDTH)
    width = basis_new.shape[0]
    start = rows_of(lax.axis_index("fsdp") * rank_local, rank_local)
    basis_new[...] = basis_t[start, pl.ds(pl.multiple_of(i * width, 128), width)].T


def fast_local(gradient, momentum, basis):
    rows, cols = gradient.shape[1:]
    rank_local = basis.shape[1]
    rank = 2 * rank_local
    levels = len(bits_of("tensor"))
    total = 2 * SLABS
    slab = rows // SLABS
    chunks = cols // CHUNK
    scale = (rows * 2 * cols * lax.axis_size("tensor") / rank) ** 0.5
    f32, bf16 = jnp.float32, jnp.bfloat16
    small = slab // 2**levels
    vmem = pl.BlockSpec(memory_space=VMEM)
    outs = [
        ((rows, cols), bf16), ((rows, cols), bf16), ((rows, rank), bf16), ((rows, rank), bf16),
        ((rank, cols), bf16), ((rank, cols), bf16), ((rank, cols), bf16), ((rank, cols), f32),
    ]
    dma = pltpu.SemaphoreType.DMA
    wide = (chunks, rank_local, CHUNK)
    made = pl.pallas_call(
        functools.partial(factors_kernel, scale),
        out_shape=tuple(VMEM(shape, kind) for shape, kind in outs),
        in_specs=[pl.BlockSpec(memory_space=ANY), pl.BlockSpec(memory_space=ANY), vmem],
        out_specs=tuple(vmem for _ in outs),
        scratch_shapes=[
            VMEM((2, slab, cols), bf16), VMEM((2, slab, cols), f32),
            VMEM((cols, rank_local), f32), VMEM((2, cols, rank), bf16),
            VMEM((total, slab, rank_local), f32), VMEM((2, rows, rank_local), f32),
            [VMEM((total, slab // 2 ** (i + 1), rank_local), f32) for i in range(levels)],
            VMEM((total, small, rank_local), f32), VMEM((total, small, rank_local), f32),
            VMEM((2, rank_local, rows), f32),
            VMEM((2,) + wide, f32), VMEM(wide, f32), VMEM(wide, f32), VMEM(wide, f32), VMEM(wide, f32), VMEM(wide, f32),
            VMEM((rank, rank), f32), VMEM((rank_local, rank), f32), VMEM((rank_local, rank), f32),
            VMEM((rank, 2 * rank), f32),
            VMEM((rank, rank), f32), VMEM((rank, rank), bf16), VMEM((rank, rank), bf16),
            VMEM((8, rank), f32), VMEM((2 * levels + 1, 8, rank), f32),
            dma((2, 2)), dma((2, FEEDS // 2)), dma((2, FEEDS // 2)), dma((2, levels, total)), dma((2, 3, total)),
            dma((2, levels, total)), dma((2, chunks)), dma((2, 3, chunks)), dma((2, chunks)), dma((2, 2)), dma((2, levels)),
        ],
        compiler_params=pltpu.CompilerParams(collective_id=0, has_side_effects=True, vmem_limit_bytes=36 << 20),
    )(gradient, momentum, basis)
    tile = slab
    return pl.pallas_call(
        outputs_kernel,
        grid=(rows // tile,),
        out_shape=(
            jax.ShapeDtypeStruct((rows, cols), bf16),
            jax.ShapeDtypeStruct((1, rows, cols), f32),
            jax.ShapeDtypeStruct((cols, rank_local), f32),
        ),
        in_specs=[vmem] * len(outs),
        out_specs=(
            pl.BlockSpec((tile, cols), lambda i: (i, 0)),
            pl.BlockSpec((1, tile, cols), lambda i: (0, i, 0)),
            pl.BlockSpec((cols * tile // rows, rank_local), lambda i: (i, 0)),
        ),
        compiler_params=pltpu.CompilerParams(vmem_limit_bytes=10 << 20),
    )(*made)


def fits(mesh):
    shape = mesh.shape
    tensor, replica = shape["tensor"], shape["replica"]
    return shape["fsdp"] == 2 and tensor > 1 and tensor & (tensor - 1) == 0 and replica % 2 == 0


def solution(mesh):
    return jax.shard_map(
        fast_local if fits(mesh) else local,
        mesh=mesh,
        in_specs=(
            P("replica", "fsdp", "tensor"),
            P("replica", "fsdp", "tensor"),
            P("tensor", "fsdp"),
        ),
        out_specs=(P("fsdp", "tensor"), P("replica", "fsdp", "tensor"), P("tensor", "fsdp")),
        check_vma=False,
    )
```

```python
import functools

import jax
import jax.numpy as jnp
from jax import lax
from jax.experimental import pallas as pl
from jax.experimental.pallas import tpu as pltpu
from jax.sharding import PartitionSpec as P

HIGHEST = lax.Precision.HIGHEST
HIGH = lax.Precision.HIGH
BLOCK = 16


def mm(a, b, precision):
    return jnp.dot(a, b, precision=precision, preferred_element_type=jnp.float32)


def pick(parts, index):
    return lax.dynamic_index_in_dim(parts, index, 0, keepdims=False)


def shift(x, axis, step):
    n = lax.axis_size(axis)
    return lax.ppermute(x, axis, [(i, (i + step) % n) for i in range(n)])


def swap(x, axis, bit):
    n = lax.axis_size(axis)
    return lax.ppermute(x, axis, [(i, i ^ bit) for i in range(n)])


def bits_of(axis):
    n = lax.axis_size(axis)
    bits, bit = [], 1
    while bit < n:
        bits.append(bit)
        bit *= 2
    return bits


def halve(x, axis, bits):
    for bit in bits:
        upper = (lax.axis_index(axis) // bit) % 2
        parts = x.reshape(2, x.shape[0] // 2, x.shape[1])
        x = pick(parts, upper) + swap(pick(parts, 1 - upper), axis, bit)
    return x


def double(x, axis, bits):
    for bit in reversed(bits):
        upper = (lax.axis_index(axis) // bit) % 2 == 1
        other = swap(x, axis, bit)
        x = jnp.concatenate([jnp.where(upper, other, x), jnp.where(upper, x, other)], axis=0)
    return x


def ring_scatter(x, axis):
    n = lax.axis_size(axis)
    me = lax.axis_index(axis)
    parts = x.reshape(n, 2, x.shape[0] // (2 * n), x.shape[1])
    up, down = parts[:, 0], parts[:, 1]
    a, b = pick(up, (me + n - 1) % n), pick(down, (me + 1) % n)
    for step in range(n - 1):
        a = shift(a, axis, 1) + pick(up, (me + 2 * n - step - 2) % n)
        b = shift(b, axis, n - 1) + pick(down, (me + step + 2) % n)
    return jnp.concatenate([a, b], axis=0)


def ring_gather(x, axis):
    n = lax.axis_size(axis)
    me = lax.axis_index(axis)
    half = x.shape[0] // 2
    a, b = x[:half], x[half:]
    out = jnp.zeros((n, 2, half, x.shape[1]), x.dtype)

    def put(out, value, chunk, side):
        return lax.dynamic_update_slice(out, value[None, None], (chunk, side, 0, 0))

    out = put(put(out, a, me, 0), b, me, 1)
    for step in range(n - 1):
        a = shift(a, axis, 1)
        b = shift(b, axis, n - 1)
        out = put(out, a, (me + n - step - 1) % n, 0)
        out = put(out, b, (me + step + 1) % n, 1)
    return out.reshape(n * x.shape[0], x.shape[1])


def sum_over(x, axis, bits, ring):
    half = x.shape[0] // 2
    first = ring_scatter(halve(x[:half], axis, bits), ring)
    second = halve(ring_scatter(x[half:], ring), axis, bits)
    first = double(ring_gather(first, ring), axis, bits)
    second = ring_gather(double(second, axis, bits), ring)
    return jnp.concatenate([first, second], axis=0)


def invert_kernel(gram_ref, out_ref, work):
    size = gram_ref.shape[0]
    rows = lax.broadcasted_iota(jnp.int32, (size, size), 0)
    cols = lax.broadcasted_iota(jnp.int32, (size, size), 1)
    work[:, :size] = gram_ref[...]
    work[:, size:] = jnp.where(rows == cols, 1.0, 0.0).astype(jnp.float32)
    lane = lax.broadcasted_iota(jnp.int32, (BLOCK, 2 * size), 1)
    row = lax.broadcasted_iota(jnp.int32, (BLOCK, 2 * size), 0)
    below = lax.broadcasted_iota(jnp.int32, (BLOCK, 1), 0)
    for start in range(0, size, BLOCK):
        panel = work[start : start + BLOCK, :]
        for j in range(BLOCK):
            column = start + j
            factor = panel[:, column : column + 1] / panel[j : j + 1, column : column + 1]
            factor = jnp.where(below > j, factor, 0.0)
            panel = panel - factor * panel[j : j + 1, :]
        pivots = jnp.sum(jnp.where(lane == row + start, panel, 0.0), axis=1, keepdims=True)
        panel = panel / jnp.sqrt(pivots)
        out_ref[start : start + BLOCK, :] = panel[:, size:]
        if start + BLOCK < size:
            outer = lax.dot_general(
                panel[:, :size],
                panel,
                (((0,), (0,)), ((), ())),
                precision=HIGHEST,
                preferred_element_type=jnp.float32,
            )
            work[start + BLOCK :, :] = work[start + BLOCK :, :] - outer[start + BLOCK :, :]


def inverse_factor(gram, interpret=False):
    size = gram.shape[0]
    return pl.pallas_call(
        invert_kernel,
        out_shape=jax.ShapeDtypeStruct((size, size), jnp.float32),
        in_specs=[pl.BlockSpec(memory_space=pltpu.VMEM)],
        out_specs=pl.BlockSpec(memory_space=pltpu.VMEM),
        scratch_shapes=[pltpu.VMEM((size, 2 * size), jnp.float32)],
        interpret=interpret,
    )(gram)


def gather_columns(x, axis):
    for bit in bits_of(axis):
        upper = (lax.axis_index(axis) // bit) % 2 == 1
        other = swap(x, axis, bit)
        x = jnp.concatenate([jnp.where(upper, other, x), jnp.where(upper, x, other)], axis=1)
    return x


def local(gradient, momentum, basis):
    replicas = lax.axis_size("replica")
    rank_local = basis.shape[1]
    rank = rank_local * lax.axis_size("fsdp")
    rows = gradient.shape[1] * lax.axis_size("fsdp")
    columns = gradient.shape[2] * lax.axis_size("tensor")
    buffer = momentum[0] + gradient[0].astype(jnp.float32)

    left = mm(buffer, gather_columns(basis, "fsdp"), HIGH)
    bits = bits_of("tensor")
    left = halve(left, "tensor", bits[:1])
    left = sum_over(left, "tensor", bits[1:], "replica")
    left = double(left, "tensor", bits[:1]) / replicas

    gram = mm(left.T, left, HIGHEST)
    for bit in bits_of("fsdp"):
        gram = gram + swap(gram, "fsdp", bit)
    ortho = mm(left, inverse_factor(gram).T, HIGHEST)

    right = mm(buffer.T, ortho, HIGH)
    right = sum_over(right, "fsdp", bits_of("fsdp"), "replica") / replicas
    squares = jnp.sum(right * right, axis=0, keepdims=True)
    for bit in bits_of("tensor"):
        squares = squares + swap(squares, "tensor", bit)
    norms = jnp.sqrt(squares + 1e-12)
    basis_full = right / norms
    lowrank = mm(ortho, right.T, lax.Precision.DEFAULT)
    momentum_new = (buffer - 0.05 * lowrank)[None]
    scale = (rows * columns / rank) ** 0.5
    update = (scale * mm(ortho, basis_full.T, HIGH)).astype(jnp.bfloat16)
    offset = lax.axis_index("fsdp") * rank_local
    basis_new = lax.dynamic_slice_in_dim(basis_full, offset, rank_local, 1)
    return (update, momentum_new, basis_new)

MESH = pl.DeviceIdType.MESH
SLABS = 8
PAIR = 2
FEEDS = 8
CHUNK = 128
WIDTH = 256
EVERY = 2
SECOND = 18
NEAR = 2
FAR = 5
HOP = 3
FEED = 5
MEET = 5
RATE = 1
EARLY = 10
PANEL = 16
VMEM = pltpu.VMEM
ANY = pl.ANY


def dot(a, b, precision=None):
    return jnp.dot(a, b, precision=precision, preferred_element_type=jnp.float32)


def split(x):
    high = x.astype(jnp.bfloat16)
    return high, (x - high.astype(jnp.float32)).astype(jnp.bfloat16)


def rows_of(start, size, unit=8):
    return pl.ds(pl.multiple_of(start, unit), size)


class Line:
    def __init__(self):
        self.n = lax.axis_size("replica")
        self.half = self.n // 2
        me = lax.axis_index("replica")
        low = me < self.half
        self.me = me
        self.depth = jnp.where(low, me, self.n - 1 - me)
        self.inward = {"replica": jnp.where(low, me + 1, me - 1)}
        outward = jnp.where(low, me - 1, me + 1)
        self.outward = {"replica": jnp.where(self.depth > 0, outward, self.inward["replica"])}


def remote(src, dst, send, recv, device):
    return pltpu.make_async_remote_copy(
        src_ref=src, dst_ref=dst, send_sem=send, recv_sem=recv, device_id=device, device_id_type=MESH
    )


def outer(a, b):
    return lax.dot_general(
        a, b, (((0,), (0,)), ((), ())), precision=HIGHEST, preferred_element_type=jnp.float32
    )


def eliminate(panel, start):
    size = panel.shape[1] // 2
    lanes = 128
    columns = [jnp.broadcast_to(panel[:, start + c : start + c + 1], (PANEL, lanes)) for c in range(PANEL)]
    tiles = [panel[:, k : k + lanes] for k in range(0, 2 * size, lanes)]
    live = [k for k in range(len(tiles)) if start < (k + 1) * lanes and k * lanes < size + start + PANEL]
    below = lax.broadcasted_iota(jnp.int32, (PANEL, lanes), 0)
    pivots = jnp.zeros((PANEL, lanes), jnp.float32)
    for j in range(PANEL):
        pivot = jnp.broadcast_to(columns[j][j : j + 1, :], (PANEL, lanes))
        pivots = jnp.where(below == j, pivot, pivots)
        factor = jnp.where(below > j, columns[j] * (1.0 / pivot), 0.0)
        for c in range(j + 1, PANEL):
            columns[c] = columns[c] - factor * columns[c][j : j + 1, :]
        for k in live:
            tiles[k] = tiles[k] - factor * tiles[k][j : j + 1, :]
    root = 1.0 / jnp.sqrt(pivots)
    for k in live:
        tiles[k] = tiles[k] * root
    return jnp.concatenate(tiles, axis=1)


def panel_step(work, out, start):
    size = out.shape[0]
    panel = eliminate(work[start : start + PANEL, :], start)
    out[start : start + PANEL, :] = panel[:, size:]
    after = start + PANEL
    if after < size:
        work[after : after + PANEL, :] = work[after : after + PANEL, :] - outer(panel[:, after : after + PANEL], panel)
        after += PANEL
    if after < size:
        low = after // 128 * 128
        high = size + (start + PANEL + 127) // 128 * 128
        change = outer(panel[:, low:size], panel[:, low:high])
        work[after:, low:high] = work[after:, low:high] - change[after - low :, :]


def factors_kernel(
    gradient, momentum, basis,
    hi, lo, ortho_hi, ortho_lo, lowrank, right_t, squares,
    stage_g, stage_m, other, pairs, part, left, halves, z_in, z_across, left_t,
    right, y_in, rz_in, rz_across, final, gathered, gram, gram_in, gram_peer, work, factor, factor_hi, factor_lo, whole_hi, whole_lo, norm_own, norm_in,
    load_sem, feed_sem, pass_sem, rs_sem, z_sem, ag_sem, y_sem, rz_sem, yg_sem, gram_sem, norm_sem,
):
    rows, cols = hi.shape
    rank_local = basis.shape[1]
    slab = rows // SLABS
    chunks = cols // CHUNK
    f = lax.axis_index("fsdp")
    t = lax.axis_index("tensor")
    line = Line()
    half, depth = line.half, line.depth
    bits = bits_of("tensor")
    levels = len(bits)
    peer_y = {"fsdp": 1 - f}
    peer_z = {"replica": line.me + 1 - 2 * (line.me % 2)}
    upper = [(t // bit) % 2 for bit in bits]
    peers = [{"tensor": t + bit - 2 * bit * up} for bit, up in zip(bits, upper)]
    spread = []
    for mask in range(1, lax.axis_size("tensor")):
        flips = [bit - 2 * bit * up for bit, up in zip(bits, upper) if mask // bit % 2]
        spread.append({"tensor": t + sum(flips)})
    sizes = [slab // 2**i for i in range(levels + 1)]
    offs = [0]
    for i in range(levels):
        offs.append(offs[i] + upper[i] * sizes[i + 1])
    total = 2 * SLABS

    def load(i, slot):
        at = rows_of(i * slab, slab)
        return (
            pltpu.make_async_copy(gradient.at[0, at], stage_g.at[slot], load_sem.at[0, slot]),
            pltpu.make_async_copy(momentum.at[0, at], stage_m.at[slot], load_sem.at[1, slot]),
        )

    for i in range(2):
        for copy in load(i, i):
            copy.start()

    barrier = pltpu.get_barrier_semaphore()

    def greet(device):
        pl.semaphore_signal(barrier, inc=1, device_id=device, device_id_type=MESH)

    greeted = 2 + len(spread)
    for device in [peer_y, line.inward] + spread:
        greet(device)
    if half > 1:
        @pl.when(depth > 0)
        def _():
            greet(line.outward)
    if half > 1:
        @pl.when(depth > 0)
        def _():
            pl.semaphore_wait(barrier, greeted + 1)

        @pl.when(depth == 0)
        def _():
            pl.semaphore_wait(barrier, greeted)
    else:
        pl.semaphore_wait(barrier, greeted)

    feeds = FEEDS // 2
    size = cols // FEEDS
    parity = line.me % 2

    def feed_copy(j):
        at = rows_of((parity * feeds + j) * size, size)
        return remote(basis.at[at], other.at[at], feed_sem.at[0, j], feed_sem.at[1, j], peer_y)

    def pass_copy(j, mine=True):
        at = rows_of(((parity if mine else 1 - parity) * feeds + j) * size, size)
        return remote(other.at[at], other.at[at], pass_sem.at[0, j], pass_sem.at[1, j], peer_z)

    early = chunks * EARLY // 16
    for j in range(feeds):
        feed_copy(j).start()

    right[...] = jnp.zeros_like(right)

    def prepare(src, which, i):
        at = rows_of(i * size, size, 16)
        high, low = split(src[at])
        pairs[which, at, :rank_local] = high
        pairs[which, at, rank_local:] = low

    for j in range(FEEDS):
        prepare(basis, 0, j)

    def place(q):
        return (f + q // SLABS) % 2, (q % SLABS) * slab

    def own(q, level):
        return part.at[q, rows_of(offs[level], sizes[level])]

    def rs_copy(q, i):
        away = offs[i] + (1 - upper[i]) * sizes[i + 1]
        return remote(
            part.at[q, rows_of(away, sizes[i + 1])], halves[i].at[q],
            rs_sem.at[0, i, q], rs_sem.at[1, i, q], peers[i],
        )

    def up_copy(q):
        return remote(own(q, levels), z_in.at[q], z_sem.at[0, 0, q], z_sem.at[1, 0, q], line.inward)

    def across_copy(q):
        return remote(own(q, levels), z_across.at[q], z_sem.at[0, 1, q], z_sem.at[1, 1, q], line.inward)

    def block(q, level, mine=True):
        blk, base = place(q)
        if mine:
            return left.at[blk, rows_of(base + offs[level], sizes[level])]
        at = offs[level - 1] + (1 - upper[level - 1]) * sizes[level]
        return left.at[blk, rows_of(base + at, sizes[level])]

    def back_copy(q):
        return remote(block(q, levels), block(q, levels), z_sem.at[0, 2, q], z_sem.at[1, 2, q], line.outward)

    def ag_copy(q, i, mine=True):
        ref = block(q, i + 1, mine)
        return remote(ref, ref, ag_sem.at[0, i, q], ag_sem.at[1, i, q], peers[i])

    def load_slab(q):
        slot = q % 2
        for copy in load(q, slot):
            copy.wait()

        def body(b, carry):
            at = rows_of(b * 32, 32)
            high, low = split(stage_m[slot, at] + stage_g[slot, at].astype(jnp.float32))
            to = rows_of(q * slab + b * 32, 32, 16)
            hi[to] = high
            lo[to] = low
            return carry
        lax.fori_loop(0, slab // 32, body, 0)

        @pl.when(q + 2 < SLABS)
        def _():
            for copy in load(q + 2, slot):
                copy.start()

    def left_part(q):
        which = q // SLABS
        at = rows_of((q % SLABS) * slab, slab, 16)
        both = dot(hi[at], pairs[which])
        cross = dot(lo[at], pairs[which, :, :rank_local])
        part[q] = both[:, :rank_local] + both[:, rank_local:] + cross
        rs_copy(q, 0).start()

    def right_part(q):
        blk, base = place(q - PAIR + 1)
        size = PAIR * slab
        at = rows_of(base, size, 16)
        flipped = left[blk, rows_of(base, size)].T
        left_t[blk, :, pl.ds(pl.multiple_of(base, size), size)] = flipped
        high, low = split(flipped)
        stacked = jnp.concatenate([high, low], axis=0)
        which = q // SLABS
        for c in range(cols // WIDTH):
            lanes = pl.ds(c * WIDTH, WIDTH)
            both = dot(stacked, hi[at, lanes])
            both = both[:rank_local] + both[rank_local:] + dot(high, lo[at, lanes])
            for k in range(WIDTH // CHUNK):
                right[which, c * (WIDTH // CHUNK) + k] += both[:, k * CHUNK : (k + 1) * CHUNK]

    done = 2 * levels + 2 * half - 1

    def advance(q, s):
        if 1 <= s <= levels:
            rs_copy(q, s - 1).wait_recv()
            ref = own(q, s)
            ref[...] += halves[s - 1][q]
            if s < levels:
                rs_copy(q, s).start()
        u = s - levels
        if 0 <= u < half:
            @pl.when(depth == u)
            def _():
                if u > 0:
                    up_copy(q).wait_recv()
                    ref = own(q, levels)
                    ref[...] += z_in[q]
                if u < half - 1:
                    up_copy(q).start()
                else:
                    across_copy(q).start()
        v = u - half
        if 0 <= v < half:
            @pl.when(depth == half - 1 - v)
            def _():
                if v == 0:
                    across_copy(q).wait_recv()
                    block(q, levels)[...] = own(q, levels)[...] + z_across[q]
                else:
                    back_copy(q).wait_recv()
                if v < half - 1:
                    back_copy(q).start()
                ag_copy(q, levels - 1).start()
        w = s - (done - levels)
        if 1 <= w <= levels:
            i = levels - w
            ag_copy(q, i, False).wait_recv()
            if i > 0:
                ag_copy(q, i - 1).start()

    def y_copy(c):
        return remote(right.at[0, c], y_in.at[c], y_sem.at[0, c], y_sem.at[1, c], peer_y)

    spans = [0, NEAR] + [FAR] * (levels - 1) + [FAR] * (2 * half - 1) + [FAR] * (levels - 1) + [NEAR]
    delay = [sum(spans[: s + 1]) for s in range(done + 1)]

    def window(n, s):
        local = n - delay[s]
        first = (local >= 0) & (local < EVERY * SLABS) & (local % EVERY == 0)
        second = (local >= SECOND) & (local < SECOND + SLABS)
        return first | second, jnp.where(local < SECOND, local // EVERY, local - SECOND + SLABS)

    def tick(n, carry):
        for s in range(done, 0, -1):
            active, q = window(n, s)

            @pl.when(active)
            def _():
                advance(q, s)

        @pl.when((n >= FEED) & (n < FEED + 2 * feeds) & ((n - FEED) % 2 == 0))
        def _():
            feed_copy((n - FEED) // 2).wait_recv()
            pass_copy((n - FEED) // 2).start()
            prepare(other, 1, parity * feeds + (n - FEED) // 2)

        @pl.when((n < EVERY * SLABS) & (n % EVERY == 0))
        def _():
            load_slab(n // EVERY)

        @pl.when(n == SECOND)
        def _():
            for j in range(feeds):
                pass_copy(j, False).wait_recv()
                prepare(other, 1, (1 - parity) * feeds + j)

        active, q = window(n, 0)

        @pl.when(active)
        def _():
            left_part(q)

        active, q = window(n, done)

        @pl.when(active & (q % PAIR == PAIR - 1))
        def _():
            right_part(q)

        @pl.when(n == delay[done] + EVERY * (SLABS - 1))
        def _():
            for c in range(early):
                y_copy(c).start()
        return carry

    lax.fori_loop(0, SECOND + SLABS + delay[done], tick, 0)

    rank = 2 * rank_local

    span = PAIR * slab

    def gram_body(i, carry):
        lanes = pl.ds(pl.multiple_of(i * span, span), span)
        for a in range(2):
            for b in range(2):
                gram[a * rank_local : (a + 1) * rank_local, b * rank_local : (b + 1) * rank_local] += dot(
                    left_t[a, :, lanes], left[b, rows_of(i * span, span)], HIGHEST
                )
        return carry

    mine = rows_of(upper[0] * rank_local, rank_local)
    theirs = rows_of((1 - upper[0]) * rank_local, rank_local)
    gram_y = remote(gram.at[mine], gram_in, gram_sem.at[0, 0], gram_sem.at[1, 0], peer_y)

    def rup_copy(c):
        return remote(right.at[1, c], rz_in.at[c], rz_sem.at[0, 0, c], rz_sem.at[1, 0, c], line.inward)

    def racross_copy(c):
        return remote(right.at[1, c], rz_across.at[c], rz_sem.at[0, 1, c], rz_sem.at[1, 1, c], line.inward)

    def rback_copy(c):
        return remote(final.at[c], final.at[c], rz_sem.at[0, 2, c], rz_sem.at[1, 2, c], line.outward)

    def yg_copy(c):
        return remote(final.at[c], gathered.at[c], yg_sem.at[0, c], yg_sem.at[1, c], peer_y)

    def radvance(c, s):
        if s == 0:
            y_copy(c).wait_recv()
            right[1, c] += y_in[c]
        if s < half:
            @pl.when(depth == s)
            def _():
                if s > 0:
                    rup_copy(c).wait_recv()
                    right[1, c] += rz_in[c]
                if s < half - 1:
                    rup_copy(c).start()
                else:
                    racross_copy(c).start()
        v = s - half
        if 0 <= v < half:
            @pl.when(depth == half - 1 - v)
            def _():
                if v == 0:
                    racross_copy(c).wait_recv()
                    final[c] = right[1, c] + rz_across[c]
                else:
                    rback_copy(c).wait_recv()
                if v < half - 1:
                    rback_copy(c).start()
                yg_copy(c).start()

    steps = chunks + HOP * (2 * half - 1)
    panels = rank // PANEL
    gram_x = remote(gram.at[mine], gram_peer, gram_sem.at[0, 1], gram_sem.at[1, 1], peers[0])
    def ortho_part(i):
        at = pl.ds(i * 256, 256)
        value = 0.0
        for a in range(2):
            high, low = split(left[a, at])
            b = pl.ds(a * rank_local, rank_local)
            top = factor_hi[b]
            both = jnp.concatenate([high, high, low], axis=1)
            value = value + dot(both, jnp.concatenate([top, factor_lo[b], top], axis=0))
        high, low = split(value)
        ortho_hi[at] = high
        ortho_lo[at] = low

    def flip_factor():
        high, low = split(factor[...].T)
        factor_hi[...] = high
        factor_lo[...] = low
        high, low = split(factor[...])
        whole_hi[...] = high
        whole_lo[...] = low

    jobs = [functools.partial(panel_step, work, factor, p * PANEL) for p in range(panels)] + [flip_factor]
    jobs += [functools.partial(ortho_part, i) for i in range(rows // 256)]
    for n in range(steps):
        if n == 0:
            gram[...] = jnp.zeros_like(gram)
            lax.fori_loop(0, SLABS // PAIR, gram_body, 0)
            gram_y.start()
            for c in range(early, chunks):
                y_copy(c).start()
        for s in range(2 * half - 1, -1, -1):
            if 0 <= n - HOP * s < chunks:
                radvance(n - HOP * s, s)
        if n == MEET:
            gram_y.wait()
            gram[mine] += gram_in[...]
            gram_x.start()
        if n == MEET + 1:
            gram_x.wait()
            work[mine, :rank] = gram[mine]
            work[theirs, :rank] = gram_peer[...]
            at = lax.broadcasted_iota(jnp.int32, (rank, rank), 0)
            to = lax.broadcasted_iota(jnp.int32, (rank, rank), 1)
            work[:, rank:] = jnp.where(at == to, 1.0, 0.0).astype(jnp.float32)
        if n > MEET:
            for job in jobs[:RATE]:
                job()
            jobs = jobs[RATE:]
    for job in jobs:
        job()

    norm_own[...] = jnp.zeros_like(norm_own)

    def final_body(c, carry):
        several = WIDTH // CHUNK
        first, second = [], []
        for k in range(several):
            i = c * several + k
            yg_copy(i).wait_recv()
            first.append(jnp.where(f == 0, gathered[i], final[i]))
            second.append(jnp.where(f == 0, final[i], gathered[i]))
        first, second = jnp.concatenate(first, axis=1), jnp.concatenate(second, axis=1)
        high, low = split(jnp.concatenate([first, second], axis=0))
        top = whole_hi[...]
        value = dot(
            jnp.concatenate([top, top, whole_lo[...]], axis=1), jnp.concatenate([high, low, high], axis=0)
        ) * (1.0 / line.n)
        lanes = pl.ds(pl.multiple_of(c * WIDTH, WIDTH), WIDTH)
        right_t[:, lanes] = value
        lowrank[:, lanes] = (0.05 * value).astype(jnp.bfloat16)
        square = value * value
        flat = square[:, :128]
        for k in range(1, WIDTH // 128):
            flat = flat + square[:, k * 128 : (k + 1) * 128]
        norm_own[...] += jnp.sum(flat.T, axis=0, keepdims=True)
        return carry
    lax.fori_loop(0, cols // WIDTH, final_body, 0)

    copies = [
        remote(norm_own, norm_in.at[i], norm_sem.at[0, i], norm_sem.at[1, i], device)
        for i, device in enumerate(spread)
    ]
    for copy in copies:
        copy.start()
    value = norm_own[...]
    for i, copy in enumerate(copies):
        copy.wait()
        value = value + norm_in[i]
    squares[...] = value

    for j in range(feeds):
        feed_copy(j).wait_send()
        pass_copy(j).wait_send()

    def drain(q, carry):
        for i in range(levels):
            rs_copy(q, i).wait_send()
            ag_copy(q, i).wait_send()

        @pl.when(depth < half - 1)
        def _():
            up_copy(q).wait_send()

        @pl.when(depth == half - 1)
        def _():
            across_copy(q).wait_send()

        @pl.when(depth > 0)
        def _():
            back_copy(q).wait_send()
        return carry
    lax.fori_loop(0, total, drain, 0)

    def rdrain(c, carry):
        y_copy(c).wait_send()
        yg_copy(c).wait_send()

        @pl.when(depth < half - 1)
        def _():
            rup_copy(c).wait_send()

        @pl.when(depth == half - 1)
        def _():
            racross_copy(c).wait_send()

        @pl.when(depth > 0)
        def _():
            rback_copy(c).wait_send()
        return carry
    lax.fori_loop(0, chunks, rdrain, 0)


def outputs_kernel(
    scale, hi, lo, ortho_hi, ortho_lo, lowrank, right_t, squares,
    update, momentum_new, basis_new, unit, update_hi, update_lo,
):
    i = pl.program_id(0)
    tile, cols = update.shape
    width, rank_local = basis_new.shape

    @pl.when(i == 0)
    def _():
        row = jnp.sqrt(squares[0:1, :] + 1e-12)
        norms = jnp.broadcast_to(row, (128, row.shape[1])).T
        norms = jnp.concatenate([norms] * (WIDTH // 128), axis=1)
        for c in range(cols // WIDTH):
            lanes = pl.ds(c * WIDTH, WIDTH)
            value = right_t[:, lanes] / norms
            unit[:, lanes] = value
            high, low = split(scale * value)
            update_hi[:, lanes] = high
            update_lo[:, lanes] = low

    at = rows_of(i * tile, tile, 16)
    high = ortho_hi[at]
    left = jnp.concatenate([high, high, ortho_lo[at]], axis=1)
    for c in range(cols // WIDTH):
        lanes = pl.ds(c * WIDTH, WIDTH)
        buffer = hi[at, lanes].astype(jnp.float32) + lo[at, lanes].astype(jnp.float32)
        momentum_new[0, :, lanes] = buffer - dot(high, lowrank[:, lanes])
        top = update_hi[:, lanes]
        right = jnp.concatenate([top, update_lo[:, lanes], top], axis=0)
        update[:, lanes] = dot(left, right).astype(jnp.bfloat16)
    start = rows_of(lax.axis_index("fsdp") * rank_local, rank_local)
    basis_new[...] = unit[start, pl.ds(pl.multiple_of(i * width, 128), width)].T


def fast_local(gradient, momentum, basis):
    rows, cols = gradient.shape[1:]
    rank_local = basis.shape[1]
    rank = 2 * rank_local
    tensor = lax.axis_size("tensor")
    levels = len(bits_of("tensor"))
    total = 2 * SLABS
    slab = rows // SLABS
    chunks = cols // CHUNK
    scale = (rows * 2 * cols * tensor / rank) ** 0.5
    f32, bf16 = jnp.float32, jnp.bfloat16
    small = slab // 2**levels
    vmem = pl.BlockSpec(memory_space=VMEM)
    outs = [
        ((rows, cols), bf16), ((rows, cols), bf16), ((rows, rank), bf16), ((rows, rank), bf16),
        ((rank, cols), bf16), ((rank, cols), f32), ((8, rank), f32),
    ]
    dma = pltpu.SemaphoreType.DMA
    wide = (chunks, rank_local, CHUNK)
    made = pl.pallas_call(
        factors_kernel,
        out_shape=tuple(VMEM(shape, kind) for shape, kind in outs),
        in_specs=[pl.BlockSpec(memory_space=ANY), pl.BlockSpec(memory_space=ANY), vmem],
        out_specs=tuple(vmem for _ in outs),
        scratch_shapes=[
            VMEM((2, slab, cols), bf16), VMEM((2, slab, cols), f32),
            VMEM((cols, rank_local), f32), VMEM((2, cols, rank), bf16),
            VMEM((total, slab, rank_local), f32), VMEM((2, rows, rank_local), f32),
            [VMEM((total, slab // 2 ** (i + 1), rank_local), f32) for i in range(levels)],
            VMEM((total, small, rank_local), f32), VMEM((total, small, rank_local), f32),
            VMEM((2, rank_local, rows), f32),
            VMEM((2,) + wide, f32), VMEM(wide, f32), VMEM(wide, f32), VMEM(wide, f32), VMEM(wide, f32), VMEM(wide, f32),
            VMEM((rank, rank), f32), VMEM((rank_local, rank), f32), VMEM((rank_local, rank), f32),
            VMEM((rank, 2 * rank), f32), VMEM((rank, rank), f32),
            VMEM((rank, rank), bf16), VMEM((rank, rank), bf16), VMEM((rank, rank), bf16), VMEM((rank, rank), bf16),
            VMEM((8, rank), f32), VMEM((tensor - 1, 8, rank), f32),
            dma((2, 2)), dma((2, FEEDS // 2)), dma((2, FEEDS // 2)), dma((2, levels, total)), dma((2, 3, total)),
            dma((2, levels, total)), dma((2, chunks)), dma((2, 3, chunks)), dma((2, chunks)), dma((2, 2)), dma((2, tensor - 1)),
        ],
        compiler_params=pltpu.CompilerParams(collective_id=0, has_side_effects=True, vmem_limit_bytes=36 << 20),
    )(gradient, momentum, basis)
    tile = slab
    return pl.pallas_call(
        functools.partial(outputs_kernel, scale),
        grid=(rows // tile,),
        out_shape=(
            jax.ShapeDtypeStruct((rows, cols), bf16),
            jax.ShapeDtypeStruct((1, rows, cols), f32),
            jax.ShapeDtypeStruct((cols, rank_local), f32),
        ),
        in_specs=[vmem] * len(outs),
        out_specs=(
            pl.BlockSpec((tile, cols), lambda i: (i, 0)),
            pl.BlockSpec((1, tile, cols), lambda i: (0, i, 0)),
            pl.BlockSpec((cols * tile // rows, rank_local), lambda i: (i, 0)),
        ),
        scratch_shapes=[VMEM((rank, cols), f32), VMEM((rank, cols), bf16), VMEM((rank, cols), bf16)],
        compiler_params=pltpu.CompilerParams(vmem_limit_bytes=14 << 20),
    )(*made)


def fits(mesh):
    shape = mesh.shape
    tensor, replica = shape["tensor"], shape["replica"]
    return shape["fsdp"] == 2 and tensor > 1 and tensor & (tensor - 1) == 0 and replica % 2 == 0


def solution(mesh):
    return jax.shard_map(
        fast_local if fits(mesh) else local,
        mesh=mesh,
        in_specs=(
            P("replica", "fsdp", "tensor"),
            P("replica", "fsdp", "tensor"),
            P("tensor", "fsdp"),
        ),
        out_specs=(P("fsdp", "tensor"), P("replica", "fsdp", "tensor"), P("tensor", "fsdp")),
        check_vma=False,
    )
```

```python
import functools

import jax
import jax.numpy as jnp
from jax import lax
from jax.experimental import pallas as pl
from jax.experimental.pallas import tpu as pltpu
from jax.sharding import PartitionSpec as P

HIGHEST = lax.Precision.HIGHEST
HIGH = lax.Precision.HIGH
BLOCK = 16


def mm(a, b, precision):
    return jnp.dot(a, b, precision=precision, preferred_element_type=jnp.float32)


def pick(parts, index):
    return lax.dynamic_index_in_dim(parts, index, 0, keepdims=False)


def shift(x, axis, step):
    n = lax.axis_size(axis)
    return lax.ppermute(x, axis, [(i, (i + step) % n) for i in range(n)])


def swap(x, axis, bit):
    n = lax.axis_size(axis)
    return lax.ppermute(x, axis, [(i, i ^ bit) for i in range(n)])


def bits_of(axis):
    n = lax.axis_size(axis)
    bits, bit = [], 1
    while bit < n:
        bits.append(bit)
        bit *= 2
    return bits


def halve(x, axis, bits):
    for bit in bits:
        upper = (lax.axis_index(axis) // bit) % 2
        parts = x.reshape(2, x.shape[0] // 2, x.shape[1])
        x = pick(parts, upper) + swap(pick(parts, 1 - upper), axis, bit)
    return x


def double(x, axis, bits):
    for bit in reversed(bits):
        upper = (lax.axis_index(axis) // bit) % 2 == 1
        other = swap(x, axis, bit)
        x = jnp.concatenate([jnp.where(upper, other, x), jnp.where(upper, x, other)], axis=0)
    return x


def ring_scatter(x, axis):
    n = lax.axis_size(axis)
    me = lax.axis_index(axis)
    parts = x.reshape(n, 2, x.shape[0] // (2 * n), x.shape[1])
    up, down = parts[:, 0], parts[:, 1]
    a, b = pick(up, (me + n - 1) % n), pick(down, (me + 1) % n)
    for step in range(n - 1):
        a = shift(a, axis, 1) + pick(up, (me + 2 * n - step - 2) % n)
        b = shift(b, axis, n - 1) + pick(down, (me + step + 2) % n)
    return jnp.concatenate([a, b], axis=0)


def ring_gather(x, axis):
    n = lax.axis_size(axis)
    me = lax.axis_index(axis)
    half = x.shape[0] // 2
    a, b = x[:half], x[half:]
    out = jnp.zeros((n, 2, half, x.shape[1]), x.dtype)

    def put(out, value, chunk, side):
        return lax.dynamic_update_slice(out, value[None, None], (chunk, side, 0, 0))

    out = put(put(out, a, me, 0), b, me, 1)
    for step in range(n - 1):
        a = shift(a, axis, 1)
        b = shift(b, axis, n - 1)
        out = put(out, a, (me + n - step - 1) % n, 0)
        out = put(out, b, (me + step + 1) % n, 1)
    return out.reshape(n * x.shape[0], x.shape[1])


def sum_over(x, axis, bits, ring):
    half = x.shape[0] // 2
    first = ring_scatter(halve(x[:half], axis, bits), ring)
    second = halve(ring_scatter(x[half:], ring), axis, bits)
    first = double(ring_gather(first, ring), axis, bits)
    second = ring_gather(double(second, axis, bits), ring)
    return jnp.concatenate([first, second], axis=0)


def invert_kernel(gram_ref, out_ref, work):
    size = gram_ref.shape[0]
    rows = lax.broadcasted_iota(jnp.int32, (size, size), 0)
    cols = lax.broadcasted_iota(jnp.int32, (size, size), 1)
    work[:, :size] = gram_ref[...]
    work[:, size:] = jnp.where(rows == cols, 1.0, 0.0).astype(jnp.float32)
    lane = lax.broadcasted_iota(jnp.int32, (BLOCK, 2 * size), 1)
    row = lax.broadcasted_iota(jnp.int32, (BLOCK, 2 * size), 0)
    below = lax.broadcasted_iota(jnp.int32, (BLOCK, 1), 0)
    for start in range(0, size, BLOCK):
        panel = work[start : start + BLOCK, :]
        for j in range(BLOCK):
            column = start + j
            factor = panel[:, column : column + 1] / panel[j : j + 1, column : column + 1]
            factor = jnp.where(below > j, factor, 0.0)
            panel = panel - factor * panel[j : j + 1, :]
        pivots = jnp.sum(jnp.where(lane == row + start, panel, 0.0), axis=1, keepdims=True)
        panel = panel / jnp.sqrt(pivots)
        out_ref[start : start + BLOCK, :] = panel[:, size:]
        if start + BLOCK < size:
            outer = lax.dot_general(
                panel[:, :size],
                panel,
                (((0,), (0,)), ((), ())),
                precision=HIGHEST,
                preferred_element_type=jnp.float32,
            )
            work[start + BLOCK :, :] = work[start + BLOCK :, :] - outer[start + BLOCK :, :]


def inverse_factor(gram, interpret=False):
    size = gram.shape[0]
    return pl.pallas_call(
        invert_kernel,
        out_shape=jax.ShapeDtypeStruct((size, size), jnp.float32),
        in_specs=[pl.BlockSpec(memory_space=pltpu.VMEM)],
        out_specs=pl.BlockSpec(memory_space=pltpu.VMEM),
        scratch_shapes=[pltpu.VMEM((size, 2 * size), jnp.float32)],
        interpret=interpret,
    )(gram)


def gather_columns(x, axis):
    for bit in bits_of(axis):
        upper = (lax.axis_index(axis) // bit) % 2 == 1
        other = swap(x, axis, bit)
        x = jnp.concatenate([jnp.where(upper, other, x), jnp.where(upper, x, other)], axis=1)
    return x


def local(gradient, momentum, basis):
    replicas = lax.axis_size("replica")
    rank_local = basis.shape[1]
    rank = rank_local * lax.axis_size("fsdp")
    rows = gradient.shape[1] * lax.axis_size("fsdp")
    columns = gradient.shape[2] * lax.axis_size("tensor")
    buffer = momentum[0] + gradient[0].astype(jnp.float32)

    left = mm(buffer, gather_columns(basis, "fsdp"), HIGH)
    bits = bits_of("tensor")
    left = halve(left, "tensor", bits[:1])
    left = sum_over(left, "tensor", bits[1:], "replica")
    left = double(left, "tensor", bits[:1]) / replicas

    gram = mm(left.T, left, HIGHEST)
    for bit in bits_of("fsdp"):
        gram = gram + swap(gram, "fsdp", bit)
    ortho = mm(left, inverse_factor(gram).T, HIGHEST)

    right = mm(buffer.T, ortho, HIGH)
    right = sum_over(right, "fsdp", bits_of("fsdp"), "replica") / replicas
    squares = jnp.sum(right * right, axis=0, keepdims=True)
    for bit in bits_of("tensor"):
        squares = squares + swap(squares, "tensor", bit)
    norms = jnp.sqrt(squares + 1e-12)
    basis_full = right / norms
    lowrank = mm(ortho, right.T, lax.Precision.DEFAULT)
    momentum_new = (buffer - 0.05 * lowrank)[None]
    scale = (rows * columns / rank) ** 0.5
    update = (scale * mm(ortho, basis_full.T, HIGH)).astype(jnp.bfloat16)
    offset = lax.axis_index("fsdp") * rank_local
    basis_new = lax.dynamic_slice_in_dim(basis_full, offset, rank_local, 1)
    return (update, momentum_new, basis_new)

MESH = pl.DeviceIdType.MESH
SLABS = 8
PAIR = 2
FEEDS = 8
CHUNK = 128
WIDTH = 256
EVERY = 2
SECOND = 18
NEAR = 2
FAR = 5
HOP = 3
FEED = 5
MEET = 5
RATE = 1
EARLY = 10
PANEL = 16
VMEM = pltpu.VMEM
ANY = pl.ANY


def dot(a, b, precision=None):
    return jnp.dot(a, b, precision=precision, preferred_element_type=jnp.float32)


def split(x):
    high = x.astype(jnp.bfloat16)
    return high, (x - high.astype(jnp.float32)).astype(jnp.bfloat16)


def rows_of(start, size, unit=8):
    return pl.ds(pl.multiple_of(start, unit), size)


class Line:
    def __init__(self):
        self.n = lax.axis_size("replica")
        self.half = self.n // 2
        me = lax.axis_index("replica")
        low = me < self.half
        self.me = me
        self.depth = jnp.where(low, me, self.n - 1 - me)
        self.inward = {"replica": jnp.where(low, me + 1, me - 1)}
        outward = jnp.where(low, me - 1, me + 1)
        self.outward = {"replica": jnp.where(self.depth > 0, outward, self.inward["replica"])}


def remote(src, dst, send, recv, device):
    return pltpu.make_async_remote_copy(
        src_ref=src, dst_ref=dst, send_sem=send, recv_sem=recv, device_id=device, device_id_type=MESH
    )


def outer(a, b):
    return lax.dot_general(
        a, b, (((0,), (0,)), ((), ())), precision=HIGHEST, preferred_element_type=jnp.float32
    )


def eliminate(panel, start):
    size = panel.shape[1] // 2
    lanes = 128
    columns = [jnp.broadcast_to(panel[:, start + c : start + c + 1], (PANEL, lanes)) for c in range(PANEL)]
    tiles = [panel[:, k : k + lanes] for k in range(0, 2 * size, lanes)]
    live = [k for k in range(len(tiles)) if start < (k + 1) * lanes and k * lanes < size + start + PANEL]
    below = lax.broadcasted_iota(jnp.int32, (PANEL, lanes), 0)
    pivots = jnp.zeros((PANEL, lanes), jnp.float32)
    for j in range(PANEL):
        pivot = jnp.broadcast_to(columns[j][j : j + 1, :], (PANEL, lanes))
        pivots = jnp.where(below == j, pivot, pivots)
        factor = jnp.where(below > j, columns[j] * (1.0 / pivot), 0.0)
        for c in range(j + 1, PANEL):
            columns[c] = columns[c] - factor * columns[c][j : j + 1, :]
        for k in live:
            tiles[k] = tiles[k] - factor * tiles[k][j : j + 1, :]
    root = 1.0 / jnp.sqrt(pivots)
    for k in live:
        tiles[k] = tiles[k] * root
    return jnp.concatenate(tiles, axis=1)


def panel_step(work, out, start):
    size = out.shape[0]
    panel = eliminate(work[start : start + PANEL, :], start)
    out[start : start + PANEL, :] = panel[:, size:]
    after = start + PANEL
    if after < size:
        work[after : after + PANEL, :] = work[after : after + PANEL, :] - outer(panel[:, after : after + PANEL], panel)
        after += PANEL
    if after < size:
        low = after // 128 * 128
        high = size + (start + PANEL + 127) // 128 * 128
        change = outer(panel[:, low:size], panel[:, low:high])
        work[after:, low:high] = work[after:, low:high] - change[after - low :, :]


def factors_kernel(
    gradient, momentum, basis,
    hi, lo, ortho_hi, ortho_lo, lowrank, right_t, squares,
    stage_g, stage_m, other, pairs, part, left, halves, z_in, z_across, left_t,
    right, y_in, rz_in, rz_across, final, gathered, gram, gram_in, gram_peer, work, factor, factor_hi, factor_lo, whole_hi, whole_lo, norm_own, norm_in,
    load_sem, feed_sem, pass_sem, rs_sem, z_sem, ag_sem, y_sem, rz_sem, yg_sem, gram_sem, norm_sem,
):
    rows, cols = hi.shape
    rank_local = basis.shape[1]
    slab = rows // SLABS
    chunks = cols // CHUNK
    f = lax.axis_index("fsdp")
    t = lax.axis_index("tensor")
    line = Line()
    half, depth = line.half, line.depth
    bits = bits_of("tensor")
    levels = len(bits)
    peer_y = {"fsdp": 1 - f}
    peer_z = {"replica": line.me + 1 - 2 * (line.me % 2)}
    upper = [(t // bit) % 2 for bit in bits]
    peers = [{"tensor": t + bit - 2 * bit * up} for bit, up in zip(bits, upper)]
    spread = []
    for mask in range(1, lax.axis_size("tensor")):
        flips = [bit - 2 * bit * up for bit, up in zip(bits, upper) if mask // bit % 2]
        spread.append({"tensor": t + sum(flips)})
    sizes = [slab // 2**i for i in range(levels + 1)]
    offs = [0]
    for i in range(levels):
        offs.append(offs[i] + upper[i] * sizes[i + 1])
    total = 2 * SLABS

    def load(i, slot):
        at = rows_of(i * slab, slab)
        return (
            pltpu.make_async_copy(gradient.at[0, at], stage_g.at[slot], load_sem.at[0, slot]),
            pltpu.make_async_copy(momentum.at[0, at], stage_m.at[slot], load_sem.at[1, slot]),
        )

    for i in range(2):
        for copy in load(i, i):
            copy.start()

    barrier = pltpu.get_barrier_semaphore()

    def greet(device):
        pl.semaphore_signal(barrier, inc=1, device_id=device, device_id_type=MESH)

    greeted = 2 + len(spread)
    for device in [peer_y, line.inward] + spread:
        greet(device)
    if half > 1:
        @pl.when(depth > 0)
        def _():
            greet(line.outward)
    if half > 1:
        @pl.when(depth > 0)
        def _():
            pl.semaphore_wait(barrier, greeted + 1)

        @pl.when(depth == 0)
        def _():
            pl.semaphore_wait(barrier, greeted)
    else:
        pl.semaphore_wait(barrier, greeted)

    feeds = FEEDS // 2
    size = cols // FEEDS
    parity = line.me % 2

    def feed_copy(j):
        at = rows_of((parity * feeds + j) * size, size)
        return remote(basis.at[at], other.at[at], feed_sem.at[0, j], feed_sem.at[1, j], peer_y)

    def pass_copy(j, mine=True):
        at = rows_of(((parity if mine else 1 - parity) * feeds + j) * size, size)
        return remote(other.at[at], other.at[at], pass_sem.at[0, j], pass_sem.at[1, j], peer_z)

    early = chunks * EARLY // 16
    for j in range(feeds):
        feed_copy(j).start()

    right[...] = jnp.zeros_like(right)

    def prepare(src, which, i):
        at = rows_of(i * size, size, 16)
        high, low = split(src[at])
        pairs[which, at, :rank_local] = high
        pairs[which, at, rank_local:] = low

    for j in range(FEEDS):
        prepare(basis, 0, j)

    def place(q):
        return (f + q // SLABS) % 2, (q % SLABS) * slab

    def own(q, level):
        return part.at[q, rows_of(offs[level], sizes[level])]

    def rs_copy(q, i):
        away = offs[i] + (1 - upper[i]) * sizes[i + 1]
        return remote(
            part.at[q, rows_of(away, sizes[i + 1])], halves[i].at[q],
            rs_sem.at[0, i, q], rs_sem.at[1, i, q], peers[i],
        )

    def up_copy(q):
        return remote(own(q, levels), z_in.at[q], z_sem.at[0, 0, q], z_sem.at[1, 0, q], line.inward)

    def across_copy(q):
        return remote(own(q, levels), z_across.at[q], z_sem.at[0, 1, q], z_sem.at[1, 1, q], line.inward)

    def block(q, level, mine=True):
        blk, base = place(q)
        if mine:
            return left.at[blk, rows_of(base + offs[level], sizes[level])]
        at = offs[level - 1] + (1 - upper[level - 1]) * sizes[level]
        return left.at[blk, rows_of(base + at, sizes[level])]

    def back_copy(q):
        return remote(block(q, levels), block(q, levels), z_sem.at[0, 2, q], z_sem.at[1, 2, q], line.outward)

    def ag_copy(q, i, mine=True):
        ref = block(q, i + 1, mine)
        return remote(ref, ref, ag_sem.at[0, i, q], ag_sem.at[1, i, q], peers[i])

    def load_slab(q):
        slot = q % 2
        for copy in load(q, slot):
            copy.wait()

        def body(b, carry):
            at = rows_of(b * 32, 32)
            high, low = split(stage_m[slot, at] + stage_g[slot, at].astype(jnp.float32))
            to = rows_of(q * slab + b * 32, 32, 16)
            hi[to] = high
            lo[to] = low
            return carry
        lax.fori_loop(0, slab // 32, body, 0)

        @pl.when(q + 2 < SLABS)
        def _():
            for copy in load(q + 2, slot):
                copy.start()

    def left_part(q):
        which = q // SLABS
        at = rows_of((q % SLABS) * slab, slab, 16)
        both = dot(hi[at], pairs[which])
        cross = dot(lo[at], pairs[which, :, :rank_local])
        part[q] = both[:, :rank_local] + both[:, rank_local:] + cross
        rs_copy(q, 0).start()

    def right_part(q):
        blk, base = place(q - PAIR + 1)
        size = PAIR * slab
        at = rows_of(base, size, 16)
        flipped = left[blk, rows_of(base, size)].T
        left_t[blk, :, pl.ds(pl.multiple_of(base, size), size)] = flipped
        high, low = split(flipped)
        stacked = jnp.concatenate([high, low], axis=0)
        which = q // SLABS
        for c in range(cols // WIDTH):
            lanes = pl.ds(c * WIDTH, WIDTH)
            both = dot(stacked, hi[at, lanes])
            both = both[:rank_local] + both[rank_local:] + dot(high, lo[at, lanes])
            for k in range(WIDTH // CHUNK):
                right[which, c * (WIDTH // CHUNK) + k] += both[:, k * CHUNK : (k + 1) * CHUNK]

    done = 2 * levels + 2 * half - 1

    def advance(q, s):
        if 1 <= s <= levels:
            rs_copy(q, s - 1).wait_recv()
            ref = own(q, s)
            ref[...] += halves[s - 1][q]
            if s < levels:
                rs_copy(q, s).start()
        u = s - levels
        if 0 <= u < half:
            @pl.when(depth == u)
            def _():
                if u > 0:
                    up_copy(q).wait_recv()
                    ref = own(q, levels)
                    ref[...] += z_in[q]
                if u < half - 1:
                    up_copy(q).start()
                else:
                    across_copy(q).start()
        v = u - half
        if 0 <= v < half:
            @pl.when(depth == half - 1 - v)
            def _():
                if v == 0:
                    across_copy(q).wait_recv()
                    block(q, levels)[...] = own(q, levels)[...] + z_across[q]
                else:
                    back_copy(q).wait_recv()
                if v < half - 1:
                    back_copy(q).start()
                ag_copy(q, levels - 1).start()
        w = s - (done - levels)
        if 1 <= w <= levels:
            i = levels - w
            ag_copy(q, i, False).wait_recv()
            if i > 0:
                ag_copy(q, i - 1).start()

    def y_copy(c):
        return remote(right.at[0, c], y_in.at[c], y_sem.at[0, c], y_sem.at[1, c], peer_y)

    spans = [0, NEAR] + [FAR] * (levels - 1) + [FAR] * (2 * half - 1) + [FAR] * (levels - 1) + [NEAR]
    delay = [sum(spans[: s + 1]) for s in range(done + 1)]

    def window(n, s):
        local = n - delay[s]
        first = (local >= 0) & (local < EVERY * SLABS) & (local % EVERY == 0)
        second = (local >= SECOND) & (local < SECOND + SLABS)
        return first | second, jnp.where(local < SECOND, local // EVERY, local - SECOND + SLABS)

    def tick(n, carry):
        for s in range(done, 0, -1):
            active, q = window(n, s)

            @pl.when(active)
            def _():
                advance(q, s)

        @pl.when((n >= FEED) & (n < FEED + 2 * feeds) & ((n - FEED) % 2 == 0))
        def _():
            feed_copy((n - FEED) // 2).wait_recv()
            pass_copy((n - FEED) // 2).start()
            prepare(other, 1, parity * feeds + (n - FEED) // 2)

        @pl.when((n < EVERY * SLABS) & (n % EVERY == 0))
        def _():
            load_slab(n // EVERY)

        @pl.when(n == SECOND)
        def _():
            for j in range(feeds):
                pass_copy(j, False).wait_recv()
                prepare(other, 1, (1 - parity) * feeds + j)

        active, q = window(n, 0)

        @pl.when(active)
        def _():
            left_part(q)

        active, q = window(n, done)

        @pl.when(active & (q % PAIR == PAIR - 1))
        def _():
            right_part(q)

        @pl.when(n == delay[done] + EVERY * (SLABS - 1))
        def _():
            for c in range(early):
                y_copy(c).start()
        return carry

    lax.fori_loop(0, SECOND + SLABS + delay[done], tick, 0)

    rank = 2 * rank_local

    span = PAIR * slab

    def gram_body(i, carry):
        lanes = pl.ds(pl.multiple_of(i * span, span), span)
        for a in range(2):
            for b in range(2):
                gram[a * rank_local : (a + 1) * rank_local, b * rank_local : (b + 1) * rank_local] += dot(
                    left_t[a, :, lanes], left[b, rows_of(i * span, span)], HIGHEST
                )
        return carry

    mine = rows_of(upper[0] * rank_local, rank_local)
    theirs = rows_of((1 - upper[0]) * rank_local, rank_local)
    gram_y = remote(gram.at[mine], gram_in, gram_sem.at[0, 0], gram_sem.at[1, 0], peer_y)

    def rup_copy(c):
        return remote(right.at[1, c], rz_in.at[c], rz_sem.at[0, 0, c], rz_sem.at[1, 0, c], line.inward)

    def racross_copy(c):
        return remote(right.at[1, c], rz_across.at[c], rz_sem.at[0, 1, c], rz_sem.at[1, 1, c], line.inward)

    def rback_copy(c):
        return remote(final.at[c], final.at[c], rz_sem.at[0, 2, c], rz_sem.at[1, 2, c], line.outward)

    def yg_copy(c):
        return remote(final.at[c], gathered.at[c], yg_sem.at[0, c], yg_sem.at[1, c], peer_y)

    def radvance(c, s):
        if s == 0:
            y_copy(c).wait_recv()
            right[1, c] += y_in[c]
        if s < half:
            @pl.when(depth == s)
            def _():
                if s > 0:
                    rup_copy(c).wait_recv()
                    right[1, c] += rz_in[c]
                if s < half - 1:
                    rup_copy(c).start()
                else:
                    racross_copy(c).start()
        v = s - half
        if 0 <= v < half:
            @pl.when(depth == half - 1 - v)
            def _():
                if v == 0:
                    racross_copy(c).wait_recv()
                    final[c] = right[1, c] + rz_across[c]
                else:
                    rback_copy(c).wait_recv()
                if v < half - 1:
                    rback_copy(c).start()
                yg_copy(c).start()

    steps = chunks + HOP * (2 * half - 1)
    panels = rank // PANEL
    gram_x = remote(gram.at[mine], gram_peer, gram_sem.at[0, 1], gram_sem.at[1, 1], peers[0])
    def ortho_part(i):
        at = pl.ds(i * 256, 256)
        value = 0.0
        for a in range(2):
            high, low = split(left[a, at])
            b = pl.ds(a * rank_local, rank_local)
            top = factor_hi[b]
            both = jnp.concatenate([high, high, low], axis=1)
            value = value + dot(both, jnp.concatenate([top, factor_lo[b], top], axis=0))
        high, low = split(value)
        ortho_hi[at] = high
        ortho_lo[at] = low

    def flip_factor():
        high, low = split(factor[...].T)
        factor_hi[...] = high
        factor_lo[...] = low
        high, low = split(factor[...])
        whole_hi[...] = high
        whole_lo[...] = low

    jobs = [functools.partial(panel_step, work, factor, p * PANEL) for p in range(panels)] + [flip_factor]
    jobs += [functools.partial(ortho_part, i) for i in range(rows // 256)]
    for n in range(steps):
        if n == 0:
            gram[...] = jnp.zeros_like(gram)
            lax.fori_loop(0, SLABS // PAIR, gram_body, 0)
            gram_y.start()
            for c in range(early, chunks):
                y_copy(c).start()
        for s in range(2 * half - 1, -1, -1):
            if 0 <= n - HOP * s < chunks:
                radvance(n - HOP * s, s)
        if n == MEET:
            gram_y.wait()
            gram[mine] += gram_in[...]
            gram_x.start()
        if n == MEET + 1:
            gram_x.wait()
            work[mine, :rank] = gram[mine]
            work[theirs, :rank] = gram_peer[...]
            at = lax.broadcasted_iota(jnp.int32, (rank, rank), 0)
            to = lax.broadcasted_iota(jnp.int32, (rank, rank), 1)
            work[:, rank:] = jnp.where(at == to, 1.0, 0.0).astype(jnp.float32)
        if n > MEET:
            rate = RATE if n < chunks else 2 * RATE
            for job in jobs[:rate]:
                job()
            jobs = jobs[rate:]
    for job in jobs:
        job()

    norm_own[...] = jnp.zeros_like(norm_own)

    def final_body(c, carry):
        several = WIDTH // CHUNK
        first, second = [], []
        for k in range(several):
            i = c * several + k
            yg_copy(i).wait_recv()
            first.append(jnp.where(f == 0, gathered[i], final[i]))
            second.append(jnp.where(f == 0, final[i], gathered[i]))
        first, second = jnp.concatenate(first, axis=1), jnp.concatenate(second, axis=1)
        high, low = split(jnp.concatenate([first, second], axis=0))
        top = whole_hi[...]
        value = dot(
            jnp.concatenate([top, top, whole_lo[...]], axis=1), jnp.concatenate([high, low, high], axis=0)
        ) * (1.0 / line.n)
        lanes = pl.ds(pl.multiple_of(c * WIDTH, WIDTH), WIDTH)
        right_t[:, lanes] = value
        lowrank[:, lanes] = (0.05 * value).astype(jnp.bfloat16)
        square = value * value
        flat = square[:, :128]
        for k in range(1, WIDTH // 128):
            flat = flat + square[:, k * 128 : (k + 1) * 128]
        norm_own[...] += jnp.sum(flat.T, axis=0, keepdims=True)
        return carry
    lax.fori_loop(0, cols // WIDTH, final_body, 0)

    copies = [
        remote(norm_own, norm_in.at[i], norm_sem.at[0, i], norm_sem.at[1, i], device)
        for i, device in enumerate(spread)
    ]
    for copy in copies:
        copy.start()
    value = norm_own[...]
    for i, copy in enumerate(copies):
        copy.wait()
        value = value + norm_in[i]
    squares[...] = value

    for j in range(feeds):
        feed_copy(j).wait_send()
        pass_copy(j).wait_send()

    def drain(q, carry):
        for i in range(levels):
            rs_copy(q, i).wait_send()
            ag_copy(q, i).wait_send()

        @pl.when(depth < half - 1)
        def _():
            up_copy(q).wait_send()

        @pl.when(depth == half - 1)
        def _():
            across_copy(q).wait_send()

        @pl.when(depth > 0)
        def _():
            back_copy(q).wait_send()
        return carry
    lax.fori_loop(0, total, drain, 0)

    def rdrain(c, carry):
        y_copy(c).wait_send()
        yg_copy(c).wait_send()

        @pl.when(depth < half - 1)
        def _():
            rup_copy(c).wait_send()

        @pl.when(depth == half - 1)
        def _():
            racross_copy(c).wait_send()

        @pl.when(depth > 0)
        def _():
            rback_copy(c).wait_send()
        return carry
    lax.fori_loop(0, chunks, rdrain, 0)


def outputs_kernel(
    scale, hi, lo, ortho_hi, ortho_lo, lowrank, right_t, squares,
    update, momentum_new, basis_new, unit, update_hi, update_lo,
):
    i = pl.program_id(0)
    tile, cols = update.shape
    width, rank_local = basis_new.shape

    @pl.when(i == 0)
    def _():
        row = jnp.sqrt(squares[0:1, :] + 1e-12)
        norms = jnp.broadcast_to(row, (128, row.shape[1])).T
        norms = jnp.concatenate([norms] * (WIDTH // 128), axis=1)
        for c in range(cols // WIDTH):
            lanes = pl.ds(c * WIDTH, WIDTH)
            value = right_t[:, lanes] / norms
            unit[:, lanes] = value
            high, low = split(scale * value)
            update_hi[:, lanes] = high
            update_lo[:, lanes] = low

    at = rows_of(i * tile, tile, 16)
    high = ortho_hi[at]
    left = jnp.concatenate([high, high, ortho_lo[at]], axis=1)
    for c in range(cols // WIDTH):
        lanes = pl.ds(c * WIDTH, WIDTH)
        buffer = hi[at, lanes].astype(jnp.float32) + lo[at, lanes].astype(jnp.float32)
        momentum_new[0, :, lanes] = buffer - dot(high, lowrank[:, lanes])
        top = update_hi[:, lanes]
        right = jnp.concatenate([top, update_lo[:, lanes], top], axis=0)
        update[:, lanes] = dot(left, right).astype(jnp.bfloat16)
    start = rows_of(lax.axis_index("fsdp") * rank_local, rank_local)
    basis_new[...] = unit[start, pl.ds(pl.multiple_of(i * width, 128), width)].T


def fast_local(gradient, momentum, basis):
    rows, cols = gradient.shape[1:]
    rank_local = basis.shape[1]
    rank = 2 * rank_local
    tensor = lax.axis_size("tensor")
    levels = len(bits_of("tensor"))
    total = 2 * SLABS
    slab = rows // SLABS
    chunks = cols // CHUNK
    scale = (rows * 2 * cols * tensor / rank) ** 0.5
    f32, bf16 = jnp.float32, jnp.bfloat16
    small = slab // 2**levels
    vmem = pl.BlockSpec(memory_space=VMEM)
    outs = [
        ((rows, cols), bf16), ((rows, cols), bf16), ((rows, rank), bf16), ((rows, rank), bf16),
        ((rank, cols), bf16), ((rank, cols), f32), ((8, rank), f32),
    ]
    dma = pltpu.SemaphoreType.DMA
    wide = (chunks, rank_local, CHUNK)
    made = pl.pallas_call(
        factors_kernel,
        out_shape=tuple(VMEM(shape, kind) for shape, kind in outs),
        in_specs=[pl.BlockSpec(memory_space=ANY), pl.BlockSpec(memory_space=ANY), vmem],
        out_specs=tuple(vmem for _ in outs),
        scratch_shapes=[
            VMEM((2, slab, cols), bf16), VMEM((2, slab, cols), f32),
            VMEM((cols, rank_local), f32), VMEM((2, cols, rank), bf16),
            VMEM((total, slab, rank_local), f32), VMEM((2, rows, rank_local), f32),
            [VMEM((total, slab // 2 ** (i + 1), rank_local), f32) for i in range(levels)],
            VMEM((total, small, rank_local), f32), VMEM((total, small, rank_local), f32),
            VMEM((2, rank_local, rows), f32),
            VMEM((2,) + wide, f32), VMEM(wide, f32), VMEM(wide, f32), VMEM(wide, f32), VMEM(wide, f32), VMEM(wide, f32),
            VMEM((rank, rank), f32), VMEM((rank_local, rank), f32), VMEM((rank_local, rank), f32),
            VMEM((rank, 2 * rank), f32), VMEM((rank, rank), f32),
            VMEM((rank, rank), bf16), VMEM((rank, rank), bf16), VMEM((rank, rank), bf16), VMEM((rank, rank), bf16),
            VMEM((8, rank), f32), VMEM((tensor - 1, 8, rank), f32),
            dma((2, 2)), dma((2, FEEDS // 2)), dma((2, FEEDS // 2)), dma((2, levels, total)), dma((2, 3, total)),
            dma((2, levels, total)), dma((2, chunks)), dma((2, 3, chunks)), dma((2, chunks)), dma((2, 2)), dma((2, tensor - 1)),
        ],
        compiler_params=pltpu.CompilerParams(collective_id=0, has_side_effects=True, vmem_limit_bytes=36 << 20),
    )(gradient, momentum, basis)
    tile = slab
    return pl.pallas_call(
        functools.partial(outputs_kernel, scale),
        grid=(rows // tile,),
        out_shape=(
            jax.ShapeDtypeStruct((rows, cols), bf16),
            jax.ShapeDtypeStruct((1, rows, cols), f32),
            jax.ShapeDtypeStruct((cols, rank_local), f32),
        ),
        in_specs=[vmem] * len(outs),
        out_specs=(
            pl.BlockSpec((tile, cols), lambda i: (i, 0)),
            pl.BlockSpec((1, tile, cols), lambda i: (0, i, 0)),
            pl.BlockSpec((cols * tile // rows, rank_local), lambda i: (i, 0)),
        ),
        scratch_shapes=[VMEM((rank, cols), f32), VMEM((rank, cols), bf16), VMEM((rank, cols), bf16)],
        compiler_params=pltpu.CompilerParams(vmem_limit_bytes=14 << 20),
    )(*made)


def fits(mesh):
    shape = mesh.shape
    tensor, replica = shape["tensor"], shape["replica"]
    return shape["fsdp"] == 2 and tensor > 1 and tensor & (tensor - 1) == 0 and replica % 2 == 0


def solution(mesh):
    return jax.shard_map(
        fast_local if fits(mesh) else local,
        mesh=mesh,
        in_specs=(
            P("replica", "fsdp", "tensor"),
            P("replica", "fsdp", "tensor"),
            P("tensor", "fsdp"),
        ),
        out_specs=(P("fsdp", "tensor"), P("replica", "fsdp", "tensor"), P("tensor", "fsdp")),
        check_vma=False,
    )
```
